256 devices in a mesh: dom: 32 (over x, y, core), pair: 8 (over z).
Axes of the slice: x: 4, y: 4, z: 8, core: 2. Of those that a mesh axis runs over, the one named last changes fastest.
Arguments:
- occupied: bfloat16 [12, 128, 256, 128], P(None, 'dom'), may hold values from -6 to 6
- virtual: bfloat16 [12, 128, 256, 128], P(None, 'dom'), may hold values from -6 to 6
- pair_ids: int32 [32, 2], P('pair'), may hold values from 0 to 11
Outputs:
- potentials: bfloat16 [32, 128, 256, 128], P('pair', 'dom')
- panel: float32 [32, 32], P('dom', 'pair')
The draws below stay inside these ranges and needn't reach their ends.
Inputs may be any that keep to these rules, and one draw needn't show every extreme that they name: `pair_ids`: each row holds an occupied orbital's index and a virtual orbital's index.
All inputs are finite; a program needn't handle non-finite values.
Results may differ from the reference program's by a relative error of at most 0.001.
Values may be sent and summed in bfloat16 or wider, within the bound.
A program may use at most 128 MiB of HBM per device.

```python
import math
import jax
import jax.numpy as jnp
from jax import lax

NY = 256
NZ = 128
PAIR_DEV = 4
ORBS = 12
NX = 128
NPAIR = 32
CELLS = 4194304
N_PAIR = 8


def orbital_field(key, count):
    keys = jax.random.split(key, 6)
    xs = jnp.arange(NX, dtype=jnp.float32)[None, :, None, None]
    ys = jnp.arange(NY, dtype=jnp.float32)[None, None, :, None]
    zs = jnp.arange(NZ, dtype=jnp.float32)[None, None, None, :]
    waves = jax.random.uniform(keys[0], (count, 3), minval=0.15, maxval=0.6)
    turns = jnp.where(jax.random.bernoulli(keys[1], 0.5, (count, 3)), 1.0, -1.0)
    rates = waves * turns
    phase = jax.random.uniform(keys[2], (count,), minval=-math.pi, maxval=math.pi)
    angle = rates[:, 0, None, None, None] * xs + rates[:, 1, None, None, None] * ys
    angle = angle + rates[:, 2, None, None, None] * zs + phase[:, None, None, None]
    amplitude = jax.random.uniform(keys[3], (count,), minval=0.6, maxval=1.4)
    noise = 0.7 * jax.random.truncated_normal(keys[5], -4.0, 4.0, (count, NX, NY, NZ))
    field = amplitude[:, None, None, None] * jnp.cos(angle) + noise
    return field.astype(jnp.float32).astype(jnp.bfloat16)


def draw_occupied(key, part):
    return orbital_field(jax.random.fold_in(key, 11), ORBS)


def draw_virtual(key, part):
    return orbital_field(jax.random.fold_in(key, 23), ORBS)


def touch_ends(array, own_key, smallest, largest):
    shape = array.shape
    index_at = [jax.random.randint(jax.random.fold_in(own_key, axis), (), 0, shape[axis]) for axis in range(len(shape))]
    array = array.at[tuple(index_at)].set(smallest)
    longest = shape.index(max(shape))
    index_at[longest] = (index_at[longest] + 1) % shape[longest]
    return array.at[tuple(index_at)].set(largest)


def setup_inputs(seed: int = 0) -> dict:
    arg_keys = jax.random.split(jax.random.key(seed), 4)
    return {
        "occupied": draw_occupied(jax.random.fold_in(arg_keys[3], 71), 0),
        "virtual": draw_virtual(jax.random.fold_in(arg_keys[3], 71), 0),
        "pair_ids": touch_ends(jax.random.randint(arg_keys[2], (NPAIR, 2), 0, ORBS), jax.random.fold_in(arg_keys[2], 1), 0, ORBS - 1).astype(jnp.int32),
    }


relax_step = 0.8 / 6.0
highest = lax.Precision.HIGHEST

def operate(field):
    padded = jnp.pad(field, ((0, 0), (1, 1), (1, 1), (1, 1)))
    beside = padded[:, 2:, 1:-1, 1:-1] + padded[:, :-2, 1:-1, 1:-1]
    beside = beside + padded[:, 1:-1, 2:, 1:-1] + padded[:, 1:-1, :-2, 1:-1]
    beside = beside + padded[:, 1:-1, 1:-1, 2:] + padded[:, 1:-1, 1:-1, :-2]
    return 6.0 * field - beside

def smooth(field, source):
    return field + relax_step * (source - operate(field))

def restrict(field):
    count, sx, sy, sz = field.shape
    blocks = field.reshape(count, sx // 2, 2, sy // 2, 2, sz // 2, 2)
    return 0.5 * lax.optimization_barrier(jnp.sum(blocks, axis=(2, 4, 6)))

def prolong(field):
    count, sx, sy, sz = field.shape
    spread = jnp.broadcast_to(field[:, :, None, :, None, :, None], (count, sx, 2, sy, 2, sz, 2))
    return spread.reshape(count, 2 * sx, 2 * sy, 2 * sz)

def sine_table(length):
    steps = jnp.arange(length, dtype=jnp.float32) + 1.0
    return math.sqrt(2.0 / (length + 1)) * jnp.sin(math.pi * steps[:, None] * steps[None, :] / (length + 1))

def mode_diagonal(length_y, length_z):
    lam_y = 2.0 - 2.0 * jnp.cos(math.pi * (jnp.arange(length_y, dtype=jnp.float32) + 1.0) / (length_y + 1))
    lam_z = 2.0 - 2.0 * jnp.cos(math.pi * (jnp.arange(length_z, dtype=jnp.float32) + 1.0) / (length_z + 1))
    return (2.0 + lam_y[:, None] + lam_z[None, :]).reshape(length_y * length_z)

def solve_lines(right_side, diagonal):
    systems = jnp.transpose(right_side, (2, 1, 0))
    count = systems.shape[1]
    main = jnp.broadcast_to(diagonal[:, None], systems.shape[:2])
    position = jnp.arange(count, dtype=jnp.int32)
    lower = jnp.broadcast_to(jnp.where(position == 0, 0.0, -1.0).astype(jnp.float32), main.shape)
    upper = jnp.broadcast_to(jnp.where(position == count - 1, 0.0, -1.0).astype(jnp.float32), main.shape)
    solved = lax.linalg.tridiagonal_solve(lower, main, upper, systems)
    return jnp.transpose(solved, (2, 1, 0))

def coarse_solve(source):
    count, sx, sy, sz = source.shape
    table_y = sine_table(sy)
    table_z = sine_table(sz)
    spectral = jnp.einsum('pxyz,ky,lz->pxkl', source, table_y, table_z, precision=highest)
    solved = solve_lines(spectral.reshape(count, sx, sy * sz), mode_diagonal(sy, sz))
    solved = solved.reshape(count, sx, sy, sz)
    return jnp.einsum('pxkl,ky,lz->pxyz', solved, table_y, table_z, precision=highest)

def vcycle(source):
    fine = smooth(relax_step * source, source)
    middle_source = restrict(source - operate(fine))
    middle = smooth(relax_step * middle_source, middle_source)
    coarse_source = restrict(middle_source - operate(middle))
    coarse = coarse_solve(coarse_source)
    middle = smooth(smooth(middle + prolong(coarse), middle_source), middle_source)
    fine = smooth(smooth(fine + prolong(middle), source), source)
    return fine

def reference(occupied, virtual, pair_ids):
    pair_groups = pair_ids.reshape(N_PAIR, PAIR_DEV, 2)

    def density(pair_rows):
        left = jnp.take(occupied, pair_rows[:, 0], axis=0).astype(jnp.float32)
        right = jnp.take(virtual, pair_rows[:, 1], axis=0).astype(jnp.float32)
        return left * right
    potentials = lax.map(lambda pair_rows: vcycle(density(pair_rows)).astype(jnp.bfloat16), pair_groups)
    potentials = potentials.reshape(NPAIR, NX, NY, NZ)
    flat = potentials.reshape(NPAIR, NX * NY * NZ)

    def panel_rows(pair_rows):
        rho_half = density(pair_rows).astype(jnp.bfloat16).reshape(PAIR_DEV, NX * NY * NZ)
        return lax.dot_general(rho_half.astype(jnp.float32), flat.astype(jnp.float32), (((1,), (1,)), ((), ())), preferred_element_type=jnp.float32)
    panel = lax.map(panel_rows, pair_groups).reshape(NPAIR, NPAIR) / float(CELLS)
    return (potentials, panel)
```

```python
import functools
import math

import jax
import jax.numpy as jnp
import numpy as np
from jax import lax
from jax.experimental import pallas as pl
from jax.experimental.pallas import tpu as pltpu
from jax.sharding import PartitionSpec as P

MESH = pl.DeviceIdType.MESH
f32 = jnp.float32
bf16 = jnp.bfloat16

w = 0.8 / 6.0
keep = 1.0 - 0.8


def lanes_of(shape):
    return lax.broadcasted_iota(jnp.int32, shape, len(shape) - 1)


def turn(value, amount):
    return pltpu.roll(value, amount % 128, value.ndim - 1)


def beside_z(value, step):
    lane = lanes_of(value.shape)
    low = jnp.where(lane >= step, turn(value, step), 0.0)
    high = jnp.where(lane < 128 - step, turn(value, -step), 0.0)
    return low + high


def plane_sum(ref, at, first, rows, step):
    middle = ref[at + (pl.ds(first + 8, rows),)]
    above = ref[at + (pl.ds(first + 7, rows),)]
    below = ref[at + (pl.ds(first + 9, rows),)]
    return middle, above + below + beside_z(middle, step)


def fold_rows(sums, mixed, at, rows):
    even = sums[at + (pl.ds(8, rows, stride=2),)]
    odd = sums[at + (pl.ds(9, rows, stride=2),)]
    before = sums[at + (pl.ds(7, rows, stride=2),)]
    after = sums[at + (pl.ds(10, rows, stride=2),)]
    folded = even + odd
    weighted = mixed[at + (pl.ds(8, rows, stride=2),)] + mixed[at + (pl.ds(9, rows, stride=2),)]
    return folded, weighted + w * (folded + before + after)


def fold_lanes(folded, weighted, step, upper):
    lane = lanes_of(folded.shape)
    if upper:
        total = weighted + turn(weighted, step)
        low, high = turn(folded, 2 * step), turn(folded, -step)
    else:
        total = weighted + turn(weighted, -step)
        low, high = turn(folded, step), turn(folded, -2 * step)
    low = jnp.where(lane >= 2 * step, low, 0.0)
    high = jnp.where(lane < 128 - 2 * step, high, 0.0)
    return 0.5 * (total + w * (low + high))


def zero_rows(ref, lead, total):
    zeros = jnp.zeros((8, 128), f32)
    for at in np.ndindex(*lead):
        ref[at + (pl.ds(0, 8),)] = zeros
        ref[at + (pl.ds(total - 8, 8),)] = zeros


def kernel(n, groups, ids_ref, occ, vir, sy_ref, sz_ref, diag_ref, pot_ref, panel_ref,
           F, Z, Y, S0, M0, X1, FC, H, Z1, V1, S1, M1, SPEC, REC, D, INV, UP, REC2, WB, U5,
           CL, CR, F16, HL, HR, X16, BL, BR, PART, REC3, IDV, IDR, IDS,
           s1, r1, s2, r2, s3, r3, s_id, r_id, s_h, r_h, loc):
    me = lax.axis_index("dom")
    group = lax.axis_index("pair")
    barrier = pltpu.get_barrier_semaphore()

    def dom_at(i):
        return lax.rem(me + i, n)

    def pair_at(i):
        return lax.rem(group + i, groups)

    def signal_dom(i, carry):
        pl.semaphore_signal(barrier, inc=1, device_id={"dom": dom_at(i)}, device_id_type=MESH)
        return carry

    def signal_pair(i, carry):
        pl.semaphore_signal(barrier, inc=1, device_id={"pair": pair_at(i)}, device_id_type=MESH)
        return carry

    lax.fori_loop(1, n, signal_dom, 0)
    lax.fori_loop(1, groups, signal_pair, 0)

    first, last = me == 0, me == n - 1
    inner_l, inner_r = me > 0, me < n - 1
    mask_l = jnp.where(inner_l, 1.0, 0.0).astype(f32)
    mask_r = jnp.where(inner_r, 1.0, 0.0).astype(f32)

    zero_rows(F, (10, 4), 272)
    zero_rows(Z, (6, 4), 272)
    zero_rows(Y, (8, 4), 272)
    zero_rows(S0, (4,), 272)
    zero_rows(X1, (10, 2), 144)
    zero_rows(FC, (4, 2), 144)
    zero_rows(H, (8, 2), 144)
    zero_rows(Z1, (6, 2), 144)
    zero_rows(S1, (2,), 144)
    UP[pl.ds(0, 2)] = jnp.zeros((2, 2, 128), f32)
    UP[pl.ds(n + 2, 2)] = jnp.zeros((2, 2, 128), f32)
    REC[pl.ds(0, 2)] = jnp.zeros((2, 10, 128), f32)
    REC[pl.ds(n + 2, 2)] = jnp.zeros((2, 10, 128), f32)

    @pl.when(first)
    def _():
        F[2] = jnp.zeros((4, 272, 128), f32)
        HL[...] = jnp.zeros((2, 4, 256, 128), bf16)
        CL[...] = jnp.zeros((2, 128, 128), f32)
        X1[pl.ds(2, 2)] = jnp.zeros((2, 2, 144, 128), f32)

    @pl.when(last)
    def _():
        F[7] = jnp.zeros((4, 272, 128), f32)
        HR[...] = jnp.zeros((2, 4, 256, 128), bf16)
        CR[...] = jnp.zeros((2, 128, 128), f32)
        X1[pl.ds(6, 2)] = jnp.zeros((2, 2, 144, 128), f32)

    @pl.when(me < 2)
    def _():
        BL[...] = jnp.zeros((2, 2, 128, 128), bf16)

    @pl.when(me > n - 3)
    def _():
        BR[...] = jnp.zeros((2, 2, 128, 128), bf16)

    row = lax.broadcasted_iota(jnp.int32, (8, 128), 0)
    col = lax.broadcasted_iota(jnp.int32, (8, 128), 1)
    own_ids = jnp.zeros((8, 128), jnp.int32)
    for i in range(4):
        for c in range(2):
            own_ids = jnp.where((row == i) & (col == c), ids_ref[i, c], own_ids)
    IDV[...] = own_ids
    IDR[group] = own_ids

    for p in range(4):
        io, iv = ids_ref[p, 0], ids_ref[p, 1]

        def density(x, carry, p=p, io=io, iv=iv):
            rho = occ[io, x].astype(f32) * vir[iv, x].astype(f32)
            F[x + 3, p, pl.ds(8, 256)] = rho
            return carry

        lax.fori_loop(0, 4, density, 0)
        for x in (1, 2):
            F16[x - 1, p] = F[x + 3, p, pl.ds(8, 256)].astype(bf16)

    def own_sweep(p, carry):
        for r in (0, 128):
            for x in range(4):
                middle, sides = plane_sum(F, (x + 3, p), r, 128, 1)
                if x > 0:
                    sides = sides + F[x + 2, p, pl.ds(r + 8, 128)]
                if x < 3:
                    sides = sides + F[x + 4, p, pl.ds(r + 8, 128)]
                Z[x + 1, p, pl.ds(r + 8, 128)] = keep * middle + w * sides
            Z[0, p, pl.ds(r + 8, 128)] = (mask_l * w) * F[3, p, pl.ds(r + 8, 128)]
            Z[5, p, pl.ds(r + 8, 128)] = (mask_r * w) * F[6, p, pl.ds(r + 8, 128)]
        return carry

    lax.fori_loop(0, 4, own_sweep, 0)

    for q in range(-1, 3):
        def fold0(p, carry, q=q):
            for r in (0, 128):
                at = pl.ds(r + 8, 128)
                if q == -1:
                    s, far = Z[0, p, at], Z[1, p, at]
                elif q == 2:
                    s, far = Z[5, p, at], Z[4, p, at]
                else:
                    s = Z[2 * q + 1, p, at] + Z[2 * q + 2, p, at]
                    far = Z[2 * q, p, at] + Z[2 * q + 3, p, at]
                S0[p, at] = s
                M0[p, at] = (keep + 2.0 * w) * s + w * far
            return carry

        lax.fori_loop(0, 4, fold0, 0)
        for ph in range(2):
            low = fold_lanes(*fold_rows(S0, M0, (2 * ph,), 128), 1, False)
            high = fold_lanes(*fold_rows(S0, M0, (2 * ph + 1,), 128), 1, True)
            value = jnp.where(lanes_of(low.shape) % 2 == 0, low, high)
            if q == -1:
                value = value * mask_l
            if q == 2:
                value = value * mask_r
            FC[q + 1, ph, pl.ds(8, 128)] = value

    for ph in range(2):
        at = pl.ds(8, 128)
        H[1, ph, at] = (mask_l * w) * FC[0, ph, at]
        H[6, ph, at] = (mask_r * w) * FC[3, ph, at]
        for i in range(-1, 3):
            middle, sides = plane_sum(FC, (i + 1, ph), 0, 128, 2)
            if i > -1:
                sides = sides + FC[i, ph, at]
            if i < 2:
                sides = sides + FC[i + 2, ph, at]
            value = keep * middle + w * sides
            if i == -1:
                value = value * mask_l
            if i == 2:
                value = value * mask_r
            H[i + 3, ph, at] = value

    parts = []
    for q in range(-2, 3):
        for ph in range(2):
            at = pl.ds(8, 128)
            lo, hi = 2 * q, 2 * q + 1
            pick = lambda i: H[i + 3, ph, at] if -2 <= i <= 3 else None
            both = [v for v in (pick(lo), pick(hi)) if v is not None]
            ends = [v for v in (pick(lo - 1), pick(hi + 1)) if v is not None]
            s = sum(both[1:], both[0]) if both else jnp.zeros((128, 128), f32)
            far = sum(ends[1:], ends[0])
            S1[ph, at] = s
            M1[ph, at] = (keep + 2.0 * w) * s + w * far
        low = fold_lanes(*fold_rows(S1, M1, (0,), 64), 2, False)
        high = fold_lanes(*fold_rows(S1, M1, (1,), 64), 2, True)
        parts.append(jnp.where(lanes_of(low.shape) % 4 < 2, low, high))
    sy, sz = sy_ref[...], sz_ref[...]
    highest = lax.Precision.HIGHEST
    wide = jnp.dot(sy, jnp.concatenate(parts, 1), precision=highest, preferred_element_type=f32)
    tall = jnp.concatenate([wide[:, 128 * j: 128 * j + 128] for j in range(5)], 0)
    WB[...] = jnp.dot(tall, sz, precision=highest, preferred_element_type=f32)
    for d in range(n):
        for j in range(5):
            SPEC[d, pl.ds(2 * j, 2)] = WB[pl.ds(64 * j + 2 * d, 2)]
    REC[me + 2] = SPEC[me]

    pl.semaphore_wait(barrier, n - 1 + groups - 1)

    def remote(src, dst, send, recv, where):
        return pltpu.make_async_remote_copy(
            src_ref=src, dst_ref=dst, send_sem=send, recv_sem=recv, device_id=where, device_id_type=MESH
        )

    def go1(t):
        return remote(SPEC.at[t], REC.at[me + 2], s1.at[t], r1.at[me], {"dom": t})

    def come1(s):
        return remote(SPEC.at[s], REC.at[s + 2], s1.at[s], r1.at[s], {"dom": s})

    def go2(t):
        return remote(UP.at[pl.ds(t, 5)], REC2.at[me], s2.at[t], r2.at[me], {"dom": t})

    def come2(s):
        return remote(UP.at[pl.ds(s, 5)], REC2.at[s], s2.at[s], r2.at[s], {"dom": s})

    def go3(t):
        return remote(PART.at[t], REC3.at[me], s3.at[t], r3.at[me], {"dom": t})

    def come3(s):
        return remote(PART.at[s], REC3.at[s], s3.at[s], r3.at[s], {"dom": s})

    def go_id(t):
        return remote(IDV, IDR.at[group], s_id.at[t], r_id.at[group], {"pair": t})

    def come_id(s):
        return remote(IDV, IDR.at[s], s_id.at[s], r_id.at[s], {"pair": s})

    def each(count, at, build, what):
        def body(i, carry):
            getattr(build(at(i)), what)()
            return carry

        lax.fori_loop(1, count, body, 0)

    each(n, dom_at, go1, "start")
    each(groups, pair_at, go_id, "start")

    in0, in1 = pl.ds(8, 256), pl.ds(8, 128)
    halos = [
        (FC.at[3, :, in1], CL, 1),
        (FC.at[0, :, in1], CR, -1),
        (F.at[6, :, in0], F.at[2, :, in0], 1),
        (F.at[3, :, in0], F.at[7, :, in0], -1),
        (X1.at[pl.ds(4, 2), :, in1], X1.at[pl.ds(2, 2), :, in1], 1),
        (X1.at[pl.ds(4, 2), :, in1], X1.at[pl.ds(6, 2), :, in1], -1),
        (X16, BL, 2),
        (X16, BR, -2),
        (F16, HL, 1),
        (F16, HR, -1),
    ]

    def halo(k, what):
        src, dst, off = halos[k]
        outgoing = what in ("start", "wait_send")
        towards = off if outgoing else -off
        there = (me < n - towards) if towards > 0 else (me >= -towards)

        @pl.when(there)
        def _():
            copy = remote(src, dst, s_h.at[k], r_h.at[k], {"dom": lax.rem(me + off + n, n)})
            getattr(copy, what)()

    halo(0, "start")
    halo(1, "start")

    base = diag_ref[me]

    def pivot(x, before):
        value = 1.0 / (base - before)
        INV[x] = value
        return value

    lax.fori_loop(0, n, pivot, jnp.zeros((2, 128), f32))

    halo(0, "wait_recv")
    halo(1, "wait_recv")
    for ph in range(2):
        for i, side in ((0, CL), (1, CR)):
            value = FC[i + 1, ph, in1] + side[ph]
            X1[i + 4, ph, in1] = value
            X16[i, ph] = value.astype(bf16)
    for k in (4, 5, 6, 7, 2, 3, 8, 9):
        halo(k, "start")

    each(n, dom_at, come1, "wait_recv")

    def forward(x, before):
        value = before
        for j in range(5):
            value = value + REC[x + 4 - j, pl.ds(2 * j, 2)]
        value = value * INV[x]
        D[x] = value
        return value

    lax.fori_loop(0, n, forward, jnp.zeros((2, 128), f32))

    def backward(i, after):
        x = n - 1 - i
        value = D[x] + INV[x] * after
        UP[x + 2] = value
        return value

    lax.fori_loop(0, n, backward, jnp.zeros((2, 128), f32))
    REC2[me] = UP[pl.ds(me, 5)]
    each(n, dom_at, go2, "start")

    for k in (2, 3, 8, 9):
        halo(k, "wait_recv")

    def widen(p, carry):
        for x in range(2):
            F[x, p, in0] = HL[x, p].astype(f32)
            F[x + 8, p, in0] = HR[x, p].astype(f32)
        return carry

    lax.fori_loop(0, 4, widen, 0)

    def mask0(x):
        at = 4 * me + x
        return jnp.where((at >= 0) & (at < 4 * n), 1.0, 0.0).astype(f32)

    def sweep_y(i, carry):
        x, p = i // 4 - 2, lax.rem(i, 4)
        for r in (0, 128):
            at = pl.ds(r + 8, 128)
            middle, sides = plane_sum(F, (x + 3, p), r, 128, 1)
            sides = sides + F[x + 2, p, at] + F[x + 4, p, at]
            Y[x + 2, p, at] = (w * (1.0 + keep)) * middle + (w * w) * sides
        return carry

    lax.fori_loop(0, 32, sweep_y, 0)

    for k in (4, 5, 6, 7):
        halo(k, "wait_recv")
    for i in range(2):
        for ph in range(2):
            X1[i, ph, in1] = BL[i, ph].astype(f32)
            X1[i + 8, ph, in1] = BR[i, ph].astype(f32)

    each(n, dom_at, come2, "wait_recv")
    for d in range(n):
        for j in range(5):
            WB[pl.ds(64 * j + 2 * d, 2)] = REC2[d, j]
    tall = jnp.dot(WB[...], sz, precision=highest, preferred_element_type=f32)
    wide = jnp.concatenate([tall[64 * j: 64 * j + 64] for j in range(5)], 1)
    wide = jnp.dot(sy, wide, precision=highest, preferred_element_type=f32)
    for j in range(5):
        U5[j] = wide[:, 128 * j: 128 * j + 128]

    def mask1(i):
        at = 2 * me + i
        return jnp.where((at >= 0) & (at < 2 * n), 1.0, 0.0).astype(f32)

    for ph in range(2):
        for i in range(-3, 5):
            middle, sides = plane_sum(X1, (i + 4, ph), 0, 128, 2)
            sides = sides + X1[i + 3, ph, in1] + X1[i + 5, ph, in1]
            H[i + 3, ph, in1] = (w * (1.0 + keep)) * middle + (w * w) * sides
        for j in range(-2, 3):
            u = U5[j + 2]
            lane = lanes_of(u.shape)
            if ph == 0:
                spread = jnp.where(lane % 4 < 2, u, turn(u, 2))
            else:
                spread = jnp.where(lane % 4 < 2, turn(u, -2), u)
            for i in (2 * j, 2 * j + 1):
                if -3 <= i < 5:
                    for odd in (8, 9):
                        at = pl.ds(odd, 64, stride=2)
                        H[i + 3, ph, at] = H[i + 3, ph, at] + spread
        for i in (-3, -2, -1, 2, 3, 4):
            H[i + 3, ph, in1] = H[i + 3, ph, in1] * mask1(i)
        for i in range(-2, 4):
            middle, sides = plane_sum(H, (i + 3, ph), 0, 128, 2)
            sides = sides + H[i + 2, ph, in1] + H[i + 4, ph, in1]
            value = keep * middle + w * (sides + X1[i + 4, ph, in1])
            Z1[i + 2, ph, in1] = value * mask1(i)
        for i in range(-1, 3):
            middle, sides = plane_sum(Z1, (i + 2, ph), 0, 128, 2)
            sides = sides + Z1[i + 1, ph, in1] + Z1[i + 3, ph, in1]
            value = keep * middle + w * (sides + X1[i + 4, ph, in1])
            V1[i + 1, ph] = value * mask1(i)

    def add_coarse(j, carry):
        for p in range(4):
            for r in (0, 64):
                v = V1[j, p // 2, pl.ds(r, 64)]
                even = lanes_of(v.shape) % 2 == 0
                if p % 2 == 0:
                    spread = jnp.where(even, v, turn(v, 1))
                else:
                    spread = jnp.where(even, turn(v, -1), v)
                for x in range(2):
                    for odd in (8, 9):
                        at = pl.ds(2 * r + odd, 64, stride=2)
                        Y[2 * j + x, p, at] = Y[2 * j + x, p, at] + spread
        return carry

    lax.fori_loop(0, 4, add_coarse, 0)

    @pl.when(first)
    def _():
        Y[pl.ds(0, 2)] = jnp.zeros((2, 4, 272, 128), f32)

    @pl.when(last)
    def _():
        Y[pl.ds(6, 2)] = jnp.zeros((2, 4, 272, 128), f32)

    def sweep_z(i, carry):
        x, p = i // 4 - 1, lax.rem(i, 4)
        mask = mask0(x)
        for r in (0, 128):
            at = pl.ds(r + 8, 128)
            middle, sides = plane_sum(Y, (x + 2, p), r, 128, 1)
            sides = sides + Y[x + 1, p, at] + Y[x + 3, p, at]
            Z[x + 1, p, at] = (keep * middle + w * (sides + F[x + 3, p, at])) * mask
        return carry

    lax.fori_loop(0, 24, sweep_z, 0)

    def sweep_out(i, carry):
        x, p = i // 4, lax.rem(i, 4)
        for r in (0, 128):
            at = pl.ds(r + 8, 128)
            middle, sides = plane_sum(Z, (x + 1, p), r, 128, 1)
            sides = sides + Z[x, p, at] + Z[x + 2, p, at]
            value = keep * middle + w * (sides + F[x + 3, p, at])
            pot_ref[p, x, pl.ds(r, 128)] = value.astype(bf16)
        return carry

    lax.fori_loop(0, 16, sweep_out, 0)

    each(groups, pair_at, come_id, "wait_recv")
    copy = pltpu.make_async_copy(IDR, IDS, loc)
    copy.start()
    copy.wait()

    def panel_rows(g, carry):
        at_o = [IDS[g, i, 0] for i in range(4)]
        at_v = [IDS[g, i, 1] for i in range(4)]

        def cells(c, sums):
            x, r = c // 8, lax.rem(c, 8) * 32
            at = pl.ds(pl.multiple_of(r, 32), 32)
            pots = [pot_ref[q, x, at].astype(f32) for q in range(4)]
            new = []
            for i in range(4):
                rho = (occ[at_o[i], x, at] * vir[at_v[i], x, at]).astype(f32)
                for q in range(4):
                    product = rho * pots[q]
                    new.append(sums[4 * i + q] + jnp.sum(product.reshape(4, 8, 128), 0))
            return tuple(new)

        sums = lax.fori_loop(0, 32, cells, tuple(jnp.zeros((8, 128), f32) for _ in range(16)))
        for i in range(4):
            rows = [jnp.sum(sums[4 * i + q], 0, keepdims=True) for q in range(4)]
            PART[4 * g + i] = jnp.concatenate(rows, 0)
        return carry

    lax.fori_loop(0, groups, panel_rows, 0)
    REC3[me] = PART[me]
    each(n, dom_at, go3, "start")
    each(n, dom_at, come3, "wait_recv")
    total = lax.fori_loop(0, n, lambda s, t: t + REC3[s], jnp.zeros((4, 128), f32))
    total = jnp.concatenate([total, jnp.zeros((4, 128), f32)], 0)
    row_sums = lax.dot_general(
        jnp.ones((8, 128), f32), total, (((1,), (1,)), ((), ())), precision=highest, preferred_element_type=f32
    )
    panel_ref[...] = row_sums[0:1, 0:4] / float(4 * 256 * 128 * n)

    for k in range(len(halos)):
        halo(k, "wait_send")
    each(n, dom_at, go1, "wait_send")
    each(n, dom_at, go2, "wait_send")
    each(n, dom_at, go3, "wait_send")
    each(groups, pair_at, go_id, "wait_send")


def tables():
    def sines(length):
        steps = np.arange(length, dtype=np.float64) + 1.0
        return np.sqrt(2.0 / (length + 1)) * np.sin(math.pi * steps[:, None] * steps[None, :] / (length + 1))

    def lams(length):
        return 2.0 - 2.0 * np.cos(math.pi * (np.arange(length, dtype=np.float64) + 1.0) / (length + 1))

    sy = sines(64).astype(np.float32)
    sz = np.kron(sines(32), np.eye(4)).astype(np.float32)
    diag = 2.0 + lams(64)[:, None] + np.repeat(lams(32), 4)[None, :]
    return sy, sz, diag.astype(np.float32).reshape(32, 2, 128)


def solution(mesh):
    n, groups = mesh.shape["dom"], mesh.shape["pair"]
    sy, sz, diag = tables()
    dma, vm = pltpu.SemaphoreType.DMA, pltpu.VMEM
    whole = pl.BlockSpec(memory_space=pltpu.VMEM)

    def shards(occupied, virtual, pair_ids):
        return pl.pallas_call(
            functools.partial(kernel, n, groups),
            out_shape=(
                jax.ShapeDtypeStruct((4, 4, 256, 128), bf16),
                jax.ShapeDtypeStruct((1, 4), f32),
            ),
            in_specs=[pl.BlockSpec(memory_space=pltpu.SMEM)] + [whole] * 5,
            out_specs=(whole, whole),
            scratch_shapes=[
                vm((10, 4, 272, 128), f32),
                vm((6, 4, 272, 128), f32),
                vm((8, 4, 272, 128), f32),
                vm((4, 272, 128), f32),
                vm((4, 272, 128), f32),
                vm((10, 2, 144, 128), f32),
                vm((4, 2, 144, 128), f32),
                vm((8, 2, 144, 128), f32),
                vm((6, 2, 144, 128), f32),
                vm((4, 2, 128, 128), f32),
                vm((2, 144, 128), f32),
                vm((2, 144, 128), f32),
                vm((n, 10, 128), f32),
                vm((n + 4, 10, 128), f32),
                vm((n, 2, 128), f32),
                vm((n, 2, 128), f32),
                vm((n + 4, 2, 128), f32),
                vm((n, 5, 2, 128), f32),
                vm((320, 128), f32),
                vm((5, 64, 128), f32),
                vm((2, 128, 128), f32),
                vm((2, 128, 128), f32),
                vm((2, 4, 256, 128), bf16),
                vm((2, 4, 256, 128), bf16),
                vm((2, 4, 256, 128), bf16),
                vm((2, 2, 128, 128), bf16),
                vm((2, 2, 128, 128), bf16),
                vm((2, 2, 128, 128), bf16),
                vm((n, 4, 128), f32),
                vm((n, 4, 128), f32),
                vm((8, 128), jnp.int32),
                vm((groups, 8, 128), jnp.int32),
                pltpu.SMEM((groups, 8, 128), jnp.int32),
                dma((n,)), dma((n,)), dma((n,)), dma((n,)), dma((n,)), dma((n,)),
                dma((groups,)), dma((groups,)),
                dma((10,)), dma((10,)), dma(()),
            ],
            compiler_params=pltpu.CompilerParams(
                collective_id=0, has_side_effects=True, vmem_limit_bytes=56 << 20
            ),
            name="casida",
        )(pair_ids, occupied, virtual, jnp.asarray(sy), jnp.asarray(sz), jnp.asarray(diag))

    return jax.shard_map(
        shards,
        mesh=mesh,
        in_specs=(P(None, "dom", None, None), P(None, "dom", None, None), P("pair", None)),
        out_specs=(P("pair", "dom", None, None), P("dom", "pair")),
        check_vma=False,
    )
```

```python
import functools
import math

import jax
import jax.numpy as jnp
import numpy as np
from jax import lax
from jax.experimental import pallas as pl
from jax.experimental.pallas import tpu as pltpu
from jax.sharding import PartitionSpec as P

MESH = pl.DeviceIdType.MESH
f32 = jnp.float32
bf16 = jnp.bfloat16

w = 0.8 / 6.0
keep = 1.0 - 0.8


def lanes_of(shape):
    return lax.broadcasted_iota(jnp.int32, shape, len(shape) - 1)


def turn(value, amount):
    return pltpu.roll(value, amount % 128, value.ndim - 1)


def beside_z(value, step):
    lane = lanes_of(value.shape)
    low = jnp.where(lane >= step, turn(value, step), 0.0)
    high = jnp.where(lane < 128 - step, turn(value, -step), 0.0)
    return low + high


def plane_sum(ref, at, first, rows, step):
    middle = ref[at + (pl.ds(first + 8, rows),)]
    above = ref[at + (pl.ds(first + 7, rows),)]
    below = ref[at + (pl.ds(first + 9, rows),)]
    return middle, above + below + beside_z(middle, step)


def fold_rows(sums, mixed, at, rows):
    even = sums[at + (pl.ds(8, rows, stride=2),)]
    odd = sums[at + (pl.ds(9, rows, stride=2),)]
    before = sums[at + (pl.ds(7, rows, stride=2),)]
    after = sums[at + (pl.ds(10, rows, stride=2),)]
    folded = even + odd
    weighted = mixed[at + (pl.ds(8, rows, stride=2),)] + mixed[at + (pl.ds(9, rows, stride=2),)]
    return folded, weighted + w * (folded + before + after)


def fold_lanes(folded, weighted, step, upper):
    lane = lanes_of(folded.shape)
    if upper:
        total = weighted + turn(weighted, step)
        low, high = turn(folded, 2 * step), turn(folded, -step)
    else:
        total = weighted + turn(weighted, -step)
        low, high = turn(folded, step), turn(folded, -2 * step)
    low = jnp.where(lane >= 2 * step, low, 0.0)
    high = jnp.where(lane < 128 - 2 * step, high, 0.0)
    return 0.5 * (total + w * (low + high))


def zero_rows(ref, lead, total):
    zeros = jnp.zeros((8, 128), f32)
    for at in np.ndindex(*lead):
        ref[at + (pl.ds(0, 8),)] = zeros
        ref[at + (pl.ds(total - 8, 8),)] = zeros


def kernel(n, groups, ids_hbm, occ_hbm, vir_hbm, sy_ref, sz_ref, diag_ref, pot_ref, panel_ref,
           occ, vir, ids_ref, F, Z, Y, S0, M0, X1, FC, H, Z1, V1, S1, M1, SPEC, REC, D, INV, UP, REC2, WB, U5,
           CL, CR, F16, HL, HR, X16, AL, AR, BL, BR, PART, REC3, IDV, IDR, IDS,
           s1, r1, s2, r2, s3, r3, s_id, r_id, s_h, r_h, loc, in_o, in_v, in_id):
    me = lax.axis_index("dom")
    group = lax.axis_index("pair")
    barrier = pltpu.get_barrier_semaphore()

    def dom_at(i):
        return lax.rem(me + i, n)

    def pair_at(i):
        return lax.rem(group + i, groups)

    def signal_dom(i, carry):
        pl.semaphore_signal(barrier, inc=1, device_id={"dom": dom_at(i)}, device_id_type=MESH)
        return carry

    def signal_pair(i, carry):
        pl.semaphore_signal(barrier, inc=1, device_id={"pair": pair_at(i)}, device_id_type=MESH)
        return carry

    lax.fori_loop(1, n, signal_dom, 0)
    lax.fori_loop(1, groups, signal_pair, 0)

    ids_in = pltpu.make_async_copy(ids_hbm, ids_ref, in_id)
    ids_in.start()
    loads = []
    for x in range(4):
        loads.append(pltpu.make_async_copy(occ_hbm.at[:, x], occ.at[:, x], in_o.at[x]))
        loads.append(pltpu.make_async_copy(vir_hbm.at[:, x], vir.at[:, x], in_v.at[x]))
    for load in loads:
        load.start()

    first, last = me == 0, me == n - 1
    inner_l, inner_r = me > 0, me < n - 1
    mask_l = jnp.where(inner_l, 1.0, 0.0).astype(f32)
    mask_r = jnp.where(inner_r, 1.0, 0.0).astype(f32)

    zero_rows(F, (10, 4), 272)
    zero_rows(Z, (6, 4), 272)
    zero_rows(Y, (8, 4), 272)
    zero_rows(S0, (4,), 272)
    zero_rows(X1, (10, 2), 144)
    zero_rows(FC, (4, 2), 144)
    zero_rows(H, (8, 2), 144)
    zero_rows(Z1, (6, 2), 144)
    zero_rows(S1, (2,), 144)
    UP[pl.ds(0, 2)] = jnp.zeros((2, 2, 128), f32)
    UP[pl.ds(n + 2, 2)] = jnp.zeros((2, 2, 128), f32)
    REC[pl.ds(0, 2)] = jnp.zeros((2, 5, 2, 128), f32)
    REC[pl.ds(n + 2, 2)] = jnp.zeros((2, 5, 2, 128), f32)

    @pl.when(first)
    def _():
        HL[...] = jnp.zeros((3, 4, 256, 128), bf16)
        AL[...] = jnp.zeros((2, 128, 128), bf16)
        CL[...] = jnp.zeros((2, 128, 128), f32)
        X1[3] = jnp.zeros((2, 144, 128), f32)

    @pl.when(last)
    def _():
        HR[...] = jnp.zeros((3, 4, 256, 128), bf16)
        AR[...] = jnp.zeros((2, 128, 128), bf16)
        CR[...] = jnp.zeros((2, 128, 128), f32)
        X1[6] = jnp.zeros((2, 144, 128), f32)

    @pl.when(me < 2)
    def _():
        BL[...] = jnp.zeros((2, 2, 128, 128), bf16)

    @pl.when(me > n - 3)
    def _():
        BR[...] = jnp.zeros((2, 2, 128, 128), bf16)

    ids_in.wait()

    row = lax.broadcasted_iota(jnp.int32, (8, 128), 0)
    col = lax.broadcasted_iota(jnp.int32, (8, 128), 1)
    own_ids = jnp.zeros((8, 128), jnp.int32)
    for i in range(4):
        for c in range(2):
            own_ids = jnp.where((row == i) & (col == c), ids_ref[i, c], own_ids)
    IDV[...] = own_ids
    IDR[group] = own_ids

    for load in loads:
        load.wait()
    for p in range(4):
        io, iv = ids_ref[p, 0], ids_ref[p, 1]

        def density(x, carry, p=p, io=io, iv=iv):
            rho = occ[io, x].astype(f32) * vir[iv, x].astype(f32)
            F[x + 3, p, pl.ds(8, 256)] = rho
            F16[x, p] = rho.astype(bf16)
            return carry

        lax.fori_loop(0, 4, density, 0)

    pl.semaphore_wait(barrier, n - 1 + groups - 1)

    def remote(src, dst, send, recv, where):
        return pltpu.make_async_remote_copy(
            src_ref=src, dst_ref=dst, send_sem=send, recv_sem=recv, device_id=where, device_id_type=MESH
        )

    def go1(t):
        return remote(SPEC.at[t], REC.at[me + 2], s1, r1, {"dom": t})

    others = pl.ds(0, n - 1)

    def all1(what):
        part = SPEC.at[others]
        getattr(remote(part, part, s1, r1, {"dom": dom_at(1)}), what)()

    def all2(what):
        part = REC2.at[others]
        getattr(remote(part, part, s2, r2, {"dom": dom_at(1)}), what)()

    def all3(what):
        part = PART.at[others]
        getattr(remote(part, part, s3, r3, {"dom": dom_at(1)}), what)()

    def go2(t):
        return remote(UP.at[pl.ds(t, 5)], REC2.at[me], s2, r2, {"dom": t})

    def go3(t):
        return remote(PART.at[t], REC3.at[me], s3, r3, {"dom": t})

    def go_id(t):
        return remote(IDV, IDR.at[group], s_id.at[t], r_id.at[group], {"pair": t})

    def come_id(s):
        return remote(IDV, IDR.at[s], s_id.at[s], r_id.at[s], {"pair": s})

    def each(count, at, build, what):
        def body(i, carry):
            getattr(build(at(i)), what)()
            return carry

        lax.fori_loop(1, count, body, 0)

    in0, in1 = pl.ds(8, 256), pl.ds(8, 128)
    halos = [
        (FC.at[3, :, in1], CL, 1),
        (FC.at[0, :, in1], CR, -1),
        (F16.at[3], HL.at[2], 1),
        (F16.at[0], HR.at[0], -1),
        (F16.at[2], HL.at[1], 1),
        (F16.at[1], HR.at[1], -1),
        (F16.at[1], HL.at[0], 1),
        (F16.at[2], HR.at[2], -1),
        (X1.at[5, :, in1], X1.at[3, :, in1], 1),
        (X1.at[4, :, in1], X1.at[6, :, in1], -1),
        (X16.at[0], AL, 1),
        (X16.at[1], AR, -1),
        (X16, BL, 2),
        (X16, BR, -2),
    ]

    def halo(k, what):
        src, dst, off = halos[k]
        outgoing = what in ("start", "wait_send")
        towards = off if outgoing else -off
        there = (me < n - towards) if towards > 0 else (me >= -towards)

        @pl.when(there)
        def _():
            copy = remote(src, dst, s_h.at[k], r_h.at[k], {"dom": lax.rem(me + off + n, n)})
            getattr(copy, what)()

    halo(2, "start")
    halo(3, "start")

    def own_sweep(p, carry):
        for r in (0, 128):
            for x in range(4):
                middle, sides = plane_sum(F, (x + 3, p), r, 128, 1)
                if x > 0:
                    sides = sides + F[x + 2, p, pl.ds(r + 8, 128)]
                if x < 3:
                    sides = sides + F[x + 4, p, pl.ds(r + 8, 128)]
                Z[x + 1, p, pl.ds(r + 8, 128)] = keep * middle + w * sides
            Z[0, p, pl.ds(r + 8, 128)] = (mask_l * w) * F[3, p, pl.ds(r + 8, 128)]
            Z[5, p, pl.ds(r + 8, 128)] = (mask_r * w) * F[6, p, pl.ds(r + 8, 128)]
        return carry

    lax.fori_loop(0, 4, own_sweep, 0)

    for q in range(-1, 3):
        def fold0(p, carry, q=q):
            for r in (0, 128):
                at = pl.ds(r + 8, 128)
                if q == -1:
                    s, far = Z[0, p, at], Z[1, p, at]
                elif q == 2:
                    s, far = Z[5, p, at], Z[4, p, at]
                else:
                    s = Z[2 * q + 1, p, at] + Z[2 * q + 2, p, at]
                    far = Z[2 * q, p, at] + Z[2 * q + 3, p, at]
                S0[p, at] = s
                M0[p, at] = (keep + 2.0 * w) * s + w * far
            return carry

        lax.fori_loop(0, 4, fold0, 0)
        for ph in range(2):
            low = fold_lanes(*fold_rows(S0, M0, (2 * ph,), 128), 1, False)
            high = fold_lanes(*fold_rows(S0, M0, (2 * ph + 1,), 128), 1, True)
            value = jnp.where(lanes_of(low.shape) % 2 == 0, low, high)
            if q == -1:
                value = value * mask_l
            if q == 2:
                value = value * mask_r
            FC[q + 1, ph, pl.ds(8, 128)] = value

    halo(0, "start")
    halo(1, "start")

    for ph in range(2):
        at = pl.ds(8, 128)
        H[1, ph, at] = (mask_l * w) * FC[0, ph, at]
        H[6, ph, at] = (mask_r * w) * FC[3, ph, at]
        for i in range(-1, 3):
            middle, sides = plane_sum(FC, (i + 1, ph), 0, 128, 2)
            if i > -1:
                sides = sides + FC[i, ph, at]
            if i < 2:
                sides = sides + FC[i + 2, ph, at]
            value = keep * middle + w * sides
            if i == -1:
                value = value * mask_l
            if i == 2:
                value = value * mask_r
            H[i + 3, ph, at] = value

    parts = []
    for q in range(-2, 3):
        for ph in range(2):
            at = pl.ds(8, 128)
            lo, hi = 2 * q, 2 * q + 1
            pick = lambda i: H[i + 3, ph, at] if -2 <= i <= 3 else None
            both = [v for v in (pick(lo), pick(hi)) if v is not None]
            ends = [v for v in (pick(lo - 1), pick(hi + 1)) if v is not None]
            s = sum(both[1:], both[0]) if both else jnp.zeros((128, 128), f32)
            far = sum(ends[1:], ends[0])
            S1[ph, at] = s
            M1[ph, at] = (keep + 2.0 * w) * s + w * far
        low = fold_lanes(*fold_rows(S1, M1, (0,), 64), 2, False)
        high = fold_lanes(*fold_rows(S1, M1, (1,), 64), 2, True)
        parts.append(jnp.where(lanes_of(low.shape) % 4 < 2, low, high))
    sy, sz = sy_ref[...], sz_ref[...]
    highest = lax.Precision.HIGHEST
    wide = jnp.dot(sy, jnp.concatenate(parts, 1), precision=highest, preferred_element_type=f32)
    tall = jnp.concatenate([wide[:, 128 * j: 128 * j + 128] for j in range(5)], 0)
    WB[...] = jnp.dot(tall, sz, precision=highest, preferred_element_type=f32)
    for d in range(n):
        for j in range(5):
            SPEC[d, j] = WB[pl.ds(64 * j + 2 * d, 2)]
    REC[me + 2] = SPEC[me]

    each(n, dom_at, go1, "start")
    each(groups, pair_at, go_id, "start")

    halo(4, "start")
    halo(5, "start")

    base = diag_ref[me]

    def pivot(x, before):
        value = 1.0 / (base - before)
        INV[x] = value
        return value

    lax.fori_loop(0, n, pivot, jnp.zeros((2, 128), f32))

    halo(0, "wait_recv")
    halo(1, "wait_recv")
    for ph in range(2):
        for i, side in ((0, CL), (1, CR)):
            value = FC[i + 1, ph, in1] + side[ph]
            X1[i + 4, ph, in1] = value
            X16[i, ph] = value.astype(bf16)
    for k in range(8, 14):
        halo(k, "start")
    for k in (6, 7):
        halo(k, "start")

    all1("wait_recv")

    def forward(x, before):
        value = before
        for j in range(5):
            value = value + REC[x + 4 - j, j]
        value = value * INV[x]
        D[x] = value
        return value

    lax.fori_loop(0, n, forward, jnp.zeros((2, 128), f32))

    def backward(i, after):
        x = n - 1 - i
        value = D[x] + INV[x] * after
        UP[x + 2] = value
        return value

    lax.fori_loop(0, n, backward, jnp.zeros((2, 128), f32))
    REC2[me] = UP[pl.ds(me, 5)]
    each(n, dom_at, go2, "start")

    for k in range(2, 8):
        halo(k, "wait_recv")

    def widen(p, carry):
        for x in range(3):
            F[x, p, in0] = HL[x, p].astype(f32)
            F[x + 7, p, in0] = HR[x, p].astype(f32)
        return carry

    lax.fori_loop(0, 4, widen, 0)

    def mask0(x):
        at = 4 * me + x
        return jnp.where((at >= 0) & (at < 4 * n), 1.0, 0.0).astype(f32)

    def sweep_y(i, carry):
        x, p = i // 4 - 2, lax.rem(i, 4)
        for r in (0, 128):
            at = pl.ds(r + 8, 128)
            middle, sides = plane_sum(F, (x + 3, p), r, 128, 1)
            sides = sides + F[x + 2, p, at] + F[x + 4, p, at]
            Y[x + 2, p, at] = (w * (1.0 + keep)) * middle + (w * w) * sides
        return carry

    lax.fori_loop(0, 32, sweep_y, 0)

    for k in range(8, 14):
        halo(k, "wait_recv")
    for ph in range(2):
        X1[2, ph, in1] = AL[ph].astype(f32)
        X1[7, ph, in1] = AR[ph].astype(f32)
    for i in range(2):
        for ph in range(2):
            X1[i, ph, in1] = BL[i, ph].astype(f32)
            X1[i + 8, ph, in1] = BR[i, ph].astype(f32)

    all2("wait_recv")
    for d in range(n):
        for j in range(5):
            WB[pl.ds(64 * j + 2 * d, 2)] = REC2[d, j]
    tall = jnp.dot(WB[...], sz, precision=highest, preferred_element_type=f32)
    wide = jnp.concatenate([tall[64 * j: 64 * j + 64] for j in range(5)], 1)
    wide = jnp.dot(sy, wide, precision=highest, preferred_element_type=f32)
    for j in range(5):
        U5[j] = wide[:, 128 * j: 128 * j + 128]

    def mask1(i):
        at = 2 * me + i
        return jnp.where((at >= 0) & (at < 2 * n), 1.0, 0.0).astype(f32)

    for ph in range(2):
        for i in range(-3, 5):
            middle, sides = plane_sum(X1, (i + 4, ph), 0, 128, 2)
            sides = sides + X1[i + 3, ph, in1] + X1[i + 5, ph, in1]
            H[i + 3, ph, in1] = (w * (1.0 + keep)) * middle + (w * w) * sides
        for j in range(-2, 3):
            u = U5[j + 2]
            lane = lanes_of(u.shape)
            if ph == 0:
                spread = jnp.where(lane % 4 < 2, u, turn(u, 2))
            else:
                spread = jnp.where(lane % 4 < 2, turn(u, -2), u)
            for i in (2 * j, 2 * j + 1):
                if -3 <= i < 5:
                    for odd in (8, 9):
                        at = pl.ds(odd, 64, stride=2)
                        H[i + 3, ph, at] = H[i + 3, ph, at] + spread
        for i in (-3, -2, -1, 2, 3, 4):
            H[i + 3, ph, in1] = H[i + 3, ph, in1] * mask1(i)
        for i in range(-2, 4):
            middle, sides = plane_sum(H, (i + 3, ph), 0, 128, 2)
            sides = sides + H[i + 2, ph, in1] + H[i + 4, ph, in1]
            value = keep * middle + w * (sides + X1[i + 4, ph, in1])
            Z1[i + 2, ph, in1] = value * mask1(i)
        for i in range(-1, 3):
            middle, sides = plane_sum(Z1, (i + 2, ph), 0, 128, 2)
            sides = sides + Z1[i + 1, ph, in1] + Z1[i + 3, ph, in1]
            value = keep * middle + w * (sides + X1[i + 4, ph, in1])
            V1[i + 1, ph] = value * mask1(i)

    def add_coarse(j, carry):
        for p in range(4):
            for r in (0, 64):
                v = V1[j, p // 2, pl.ds(r, 64)]
                even = lanes_of(v.shape) % 2 == 0
                if p % 2 == 0:
                    spread = jnp.where(even, v, turn(v, 1))
                else:
                    spread = jnp.where(even, turn(v, -1), v)
                for x in range(2):
                    for odd in (8, 9):
                        at = pl.ds(2 * r + odd, 64, stride=2)
                        Y[2 * j + x, p, at] = Y[2 * j + x, p, at] + spread
        return carry

    lax.fori_loop(0, 4, add_coarse, 0)

    @pl.when(first)
    def _():
        Y[pl.ds(0, 2)] = jnp.zeros((2, 4, 272, 128), f32)

    @pl.when(last)
    def _():
        Y[pl.ds(6, 2)] = jnp.zeros((2, 4, 272, 128), f32)

    def sweep_z(i, carry):
        x, p = i // 4 - 1, lax.rem(i, 4)
        mask = mask0(x)
        for r in (0, 128):
            at = pl.ds(r + 8, 128)
            middle, sides = plane_sum(Y, (x + 2, p), r, 128, 1)
            sides = sides + Y[x + 1, p, at] + Y[x + 3, p, at]
            Z[x + 1, p, at] = (keep * middle + w * (sides + F[x + 3, p, at])) * mask
        return carry

    lax.fori_loop(0, 24, sweep_z, 0)

    def sweep_out(i, carry):
        x, p = i // 4, lax.rem(i, 4)
        for r in (0, 128):
            at = pl.ds(r + 8, 128)
            middle, sides = plane_sum(Z, (x + 1, p), r, 128, 1)
            sides = sides + Z[x, p, at] + Z[x + 2, p, at]
            value = keep * middle + w * (sides + F[x + 3, p, at])
            pot_ref[p, x, pl.ds(r, 128)] = value.astype(bf16)
        return carry

    lax.fori_loop(0, 16, sweep_out, 0)

    each(groups, pair_at, come_id, "wait_recv")
    copy = pltpu.make_async_copy(IDR, IDS, loc)
    copy.start()
    copy.wait()

    def panel_rows(g, carry):
        at_o = [IDS[2 * g + i // 4, i % 4, 0] for i in range(8)]
        at_v = [IDS[2 * g + i // 4, i % 4, 1] for i in range(8)]

        def cells(c, sums):
            x, r = c // 16, lax.rem(c, 16) * 16
            at = pl.ds(pl.multiple_of(r, 16), 16)
            pots = [pot_ref[q, x, at].astype(f32) for q in range(4)]
            new = []
            for i in range(8):
                rho = (occ[at_o[i], x, at] * vir[at_v[i], x, at]).astype(f32)
                for q in range(4):
                    product = rho * pots[q]
                    new.append(sums[4 * i + q] + (product[:8] + product[8:]))
            return tuple(new)

        sums = lax.fori_loop(0, 64, cells, tuple(jnp.zeros((8, 128), f32) for _ in range(32)))
        for i in range(8):
            rows = [jnp.sum(sums[4 * i + q], 0, keepdims=True) for q in range(4)]
            PART[8 * g + i] = jnp.concatenate(rows, 0)
        return carry

    lax.fori_loop(0, groups // 2, panel_rows, 0)
    REC3[me] = PART[me]
    each(n, dom_at, go3, "start")
    all3("wait_recv")
    total = lax.fori_loop(0, n, lambda s, t: t + REC3[s], jnp.zeros((4, 128), f32))
    total = jnp.concatenate([total, jnp.zeros((4, 128), f32)], 0)
    row_sums = lax.dot_general(
        jnp.ones((8, 128), f32), total, (((1,), (1,)), ((), ())), precision=highest, preferred_element_type=f32
    )
    panel_ref[...] = row_sums[0:1, 0:4] / float(4 * 256 * 128 * n)

    for k in range(len(halos)):
        halo(k, "wait_send")
    all1("wait_send")
    all2("wait_send")
    all3("wait_send")
    each(groups, pair_at, go_id, "wait_send")


def tables():
    def sines(length):
        steps = np.arange(length, dtype=np.float64) + 1.0
        return np.sqrt(2.0 / (length + 1)) * np.sin(math.pi * steps[:, None] * steps[None, :] / (length + 1))

    def lams(length):
        return 2.0 - 2.0 * np.cos(math.pi * (np.arange(length, dtype=np.float64) + 1.0) / (length + 1))

    sy = sines(64).astype(np.float32)
    sz = np.kron(sines(32), np.eye(4)).astype(np.float32)
    diag = 2.0 + lams(64)[:, None] + np.repeat(lams(32), 4)[None, :]
    return sy, sz, diag.astype(np.float32).reshape(32, 2, 128)


def solution(mesh):
    n, groups = mesh.shape["dom"], mesh.shape["pair"]
    sy, sz, diag = tables()
    dma, vm = pltpu.SemaphoreType.DMA, pltpu.VMEM
    whole = pl.BlockSpec(memory_space=pltpu.VMEM)

    def shards(occupied, virtual, pair_ids):
        return pl.pallas_call(
            functools.partial(kernel, n, groups),
            out_shape=(
                jax.ShapeDtypeStruct((4, 4, 256, 128), bf16),
                jax.ShapeDtypeStruct((1, 4), f32),
            ),
            in_specs=[pl.BlockSpec(memory_space=pl.ANY)] * 3 + [whole] * 3,
            out_specs=(whole, whole),
            scratch_shapes=[
                vm((12, 4, 256, 128), bf16),
                vm((12, 4, 256, 128), bf16),
                pltpu.SMEM((4, 2), jnp.int32),
                vm((10, 4, 272, 128), f32),
                vm((6, 4, 272, 128), f32),
                vm((8, 4, 272, 128), f32),
                vm((4, 272, 128), f32),
                vm((4, 272, 128), f32),
                vm((10, 2, 144, 128), f32),
                vm((4, 2, 144, 128), f32),
                vm((8, 2, 144, 128), f32),
                vm((6, 2, 144, 128), f32),
                vm((4, 2, 128, 128), f32),
                vm((2, 144, 128), f32),
                vm((2, 144, 128), f32),
                vm((n, 5, 2, 128), f32),
                vm((n + 4, 5, 2, 128), f32),
                vm((n, 2, 128), f32),
                vm((n, 2, 128), f32),
                vm((n + 4, 2, 128), f32),
                vm((n, 5, 2, 128), f32),
                vm((320, 128), f32),
                vm((5, 64, 128), f32),
                vm((2, 128, 128), f32),
                vm((2, 128, 128), f32),
                vm((4, 4, 256, 128), bf16),
                vm((3, 4, 256, 128), bf16),
                vm((3, 4, 256, 128), bf16),
                vm((2, 2, 128, 128), bf16),
                vm((2, 128, 128), bf16),
                vm((2, 128, 128), bf16),
                vm((2, 2, 128, 128), bf16),
                vm((2, 2, 128, 128), bf16),
                vm((n, 4, 128), f32),
                vm((n, 4, 128), f32),
                vm((8, 128), jnp.int32),
                vm((groups, 8, 128), jnp.int32),
                pltpu.SMEM((groups, 8, 128), jnp.int32),
                dma(()), dma(()), dma(()), dma(()), dma(()), dma(()),
                dma((groups,)), dma((groups,)),
                dma((14,)), dma((14,)), dma(()), dma((4,)), dma((4,)), dma(()),
            ],
            compiler_params=pltpu.CompilerParams(
                collective_id=0, has_side_effects=True, vmem_limit_bytes=56 << 20
            ),
            name="casida",
        )(pair_ids, occupied, virtual, jnp.asarray(sy), jnp.asarray(sz), jnp.asarray(diag))

    return jax.shard_map(
        shards,
        mesh=mesh,
        in_specs=(P(None, "dom", None, None), P(None, "dom", None, None), P("pair", None)),
        out_specs=(P("pair", "dom", None, None), P("dom", "pair")),
        check_vma=False,
    )
```

```python
import functools
import math

import jax
import jax.numpy as jnp
import numpy as np
from jax import lax
from jax.experimental import pallas as pl
from jax.experimental.pallas import tpu as pltpu
from jax.sharding import PartitionSpec as P

MESH = pl.DeviceIdType.MESH
f32 = jnp.float32
bf16 = jnp.bfloat16

w = 0.8 / 6.0
keep = 1.0 - 0.8


def lanes_of(shape):
    return lax.broadcasted_iota(jnp.int32, shape, len(shape) - 1)


def turn(value, amount):
    return pltpu.roll(value, amount % 128, value.ndim - 1)


def beside_z(value, step):
    lane = lanes_of(value.shape)
    low = jnp.where(lane >= step, turn(value, step), 0.0)
    high = jnp.where(lane < 128 - step, turn(value, -step), 0.0)
    return low + high


def plane_sum(ref, at, first, rows, step):
    middle = ref[at + (pl.ds(first + 8, rows),)]
    above = ref[at + (pl.ds(first + 7, rows),)]
    below = ref[at + (pl.ds(first + 9, rows),)]
    return middle, above + below + beside_z(middle, step)


def fold_rows(sums, mixed, at, rows):
    even = sums[at + (pl.ds(8, rows, stride=2),)]
    odd = sums[at + (pl.ds(9, rows, stride=2),)]
    before = sums[at + (pl.ds(7, rows, stride=2),)]
    after = sums[at + (pl.ds(10, rows, stride=2),)]
    folded = even + odd
    weighted = mixed[at + (pl.ds(8, rows, stride=2),)] + mixed[at + (pl.ds(9, rows, stride=2),)]
    return folded, weighted + w * (folded + before + after)


def fold_lanes(folded, weighted, step, upper):
    lane = lanes_of(folded.shape)
    if upper:
        total = weighted + turn(weighted, step)
        low, high = turn(folded, 2 * step), turn(folded, -step)
    else:
        total = weighted + turn(weighted, -step)
        low, high = turn(folded, step), turn(folded, -2 * step)
    low = jnp.where(lane >= 2 * step, low, 0.0)
    high = jnp.where(lane < 128 - 2 * step, high, 0.0)
    return 0.5 * (total + w * (low + high))


def zero_rows(ref, lead, total):
    zeros = jnp.zeros((8, 128), f32)
    for at in np.ndindex(*lead):
        ref[at + (pl.ds(0, 8),)] = zeros
        ref[at + (pl.ds(total - 8, 8),)] = zeros


def kernel(n, groups, ids_hbm, occ_hbm, vir_hbm, sy_ref, sz_ref, diag_ref, pot_ref, panel_ref,
           occ, vir, ids_ref, F, Z, Y, S0, M0, X1, FC, H, Z1, V1, S1, M1, SPEC, REC, D, INV, UP, REC2, WB, U5,
           CL, CR, F16, HL, HR, X16, AL, AR, BL, BR, PART, REC3, IDV, IDR, IDS,
           s1, r1, s2, r2, s3, r3, s_id, r_id, s_h, r_h, loc, in_o, in_v, in_id):
    me = lax.axis_index("dom")
    group = lax.axis_index("pair")
    barrier = pltpu.get_barrier_semaphore()

    def dom_at(i):
        return lax.rem(me + i, n)

    def pair_at(i):
        return lax.rem(group + i, groups)

    def signal_dom(i, carry):
        pl.semaphore_signal(barrier, inc=1, device_id={"dom": dom_at(i)}, device_id_type=MESH)
        return carry

    def signal_pair(i, carry):
        pl.semaphore_signal(barrier, inc=1, device_id={"pair": pair_at(i)}, device_id_type=MESH)
        return carry

    lax.fori_loop(1, n, signal_dom, 0)
    lax.fori_loop(1, groups, signal_pair, 0)

    ids_in = pltpu.make_async_copy(ids_hbm, ids_ref, in_id)
    ids_in.start()
    loads = []
    for x in range(4):
        loads.append(pltpu.make_async_copy(occ_hbm.at[:, x], occ.at[:, x], in_o.at[x]))
        loads.append(pltpu.make_async_copy(vir_hbm.at[:, x], vir.at[:, x], in_v.at[x]))
    for load in loads:
        load.start()

    first, last = me == 0, me == n - 1
    inner_l, inner_r = me > 0, me < n - 1
    mask_l = jnp.where(inner_l, 1.0, 0.0).astype(f32)
    mask_r = jnp.where(inner_r, 1.0, 0.0).astype(f32)

    zero_rows(F, (10, 4), 272)
    zero_rows(Z, (6, 4), 272)
    zero_rows(Y, (8, 4), 272)
    zero_rows(S0, (4,), 272)
    zero_rows(X1, (10, 2), 144)
    zero_rows(FC, (4, 2), 144)
    zero_rows(H, (8, 2), 144)
    zero_rows(Z1, (6, 2), 144)
    zero_rows(S1, (2,), 144)
    UP[pl.ds(0, 2)] = jnp.zeros((2, 2, 128), f32)
    UP[pl.ds(n + 2, 2)] = jnp.zeros((2, 2, 128), f32)
    REC[pl.ds(0, 2)] = jnp.zeros((2, 5, 2, 128), f32)
    REC[pl.ds(n + 2, 2)] = jnp.zeros((2, 5, 2, 128), f32)

    @pl.when(first)
    def _():
        HL[...] = jnp.zeros((3, 4, 256, 128), bf16)
        AL[...] = jnp.zeros((2, 2, 128, 128), bf16)
        BL[...] = jnp.zeros((2, 2, 128, 128), bf16)
        CL[...] = jnp.zeros((2, 128, 128), f32)

    @pl.when(last)
    def _():
        HR[...] = jnp.zeros((3, 4, 256, 128), bf16)
        AR[...] = jnp.zeros((2, 2, 128, 128), bf16)
        BR[...] = jnp.zeros((2, 2, 128, 128), bf16)
        CR[...] = jnp.zeros((2, 128, 128), f32)

    ids_in.wait()

    row = lax.broadcasted_iota(jnp.int32, (8, 128), 0)
    col = lax.broadcasted_iota(jnp.int32, (8, 128), 1)
    own_ids = jnp.zeros((8, 128), jnp.int32)
    for i in range(4):
        for c in range(2):
            own_ids = jnp.where((row == i) & (col == c), ids_ref[i, c], own_ids)
    IDV[...] = own_ids
    IDR[group] = own_ids

    for load in loads:
        load.wait()
    for p in range(4):
        io, iv = ids_ref[p, 0], ids_ref[p, 1]

        def density(x, carry, p=p, io=io, iv=iv):
            rho = occ[io, x].astype(f32) * vir[iv, x].astype(f32)
            F[x + 3, p, pl.ds(8, 256)] = rho
            F16[x, p] = rho.astype(bf16)
            return carry

        lax.fori_loop(0, 4, density, 0)


    def remote(src, dst, send, recv, where):
        return pltpu.make_async_remote_copy(
            src_ref=src, dst_ref=dst, send_sem=send, recv_sem=recv, device_id=where, device_id_type=MESH
        )

    def go1(t):
        return remote(SPEC.at[t], REC.at[me + 2], s1, r1, {"dom": t})

    others = pl.ds(0, n - 1)

    def all1(what):
        part = SPEC.at[others]
        getattr(remote(part, part, s1, r1, {"dom": dom_at(1)}), what)()

    def all2(what):
        part = REC2.at[others]
        getattr(remote(part, part, s2, r2, {"dom": dom_at(1)}), what)()

    def all3(what):
        part = PART.at[others]
        getattr(remote(part, part, s3, r3, {"dom": dom_at(1)}), what)()

    def go2(t):
        return remote(UP.at[pl.ds(t, 5)], REC2.at[me], s2, r2, {"dom": t})

    def go3(t):
        return remote(PART.at[t], REC3.at[me], s3, r3, {"dom": t})

    def go_id(t):
        return remote(IDV, IDR.at[group], s_id.at[t], r_id.at[group], {"pair": t})

    def come_id(s):
        return remote(IDV, IDR.at[s], s_id.at[s], r_id.at[s], {"pair": s})

    def each(count, at, build, what):
        def body(i, carry):
            getattr(build(at(i)), what)()
            return carry

        lax.fori_loop(1, count, body, 0)

    in0, in1 = pl.ds(8, 256), pl.ds(8, 128)
    halos = [
        (FC.at[3, :, in1], CL, 1),
        (FC.at[0, :, in1], CR, -1),
        (F16.at[3], HL.at[2], 1),
        (F16.at[0], HR.at[0], -1),
        (F16.at[2], HL.at[1], 1),
        (F16.at[1], HR.at[1], -1),
        (F16.at[1], HL.at[0], 1),
        (F16.at[2], HR.at[2], -1),
        (X16, AL, 1),
        (X16, AR, -1),
        (AL, BL, 1),
        (AR, BR, -1),
    ]

    def halo(k, what):
        src, dst, off = halos[k]
        outgoing = what in ("start", "wait_send")
        towards = off if outgoing else -off
        there = (me < n - towards) if towards > 0 else (me >= -towards)

        @pl.when(there)
        def _():
            copy = remote(src, dst, s_h.at[k], r_h.at[k], {"dom": lax.rem(me + off + n, n)})
            getattr(copy, what)()

    def own_sweep(p, carry):
        for r in (0, 128):
            for x in range(4):
                middle, sides = plane_sum(F, (x + 3, p), r, 128, 1)
                if x > 0:
                    sides = sides + F[x + 2, p, pl.ds(r + 8, 128)]
                if x < 3:
                    sides = sides + F[x + 4, p, pl.ds(r + 8, 128)]
                Z[x + 1, p, pl.ds(r + 8, 128)] = keep * middle + w * sides
            Z[0, p, pl.ds(r + 8, 128)] = (mask_l * w) * F[3, p, pl.ds(r + 8, 128)]
            Z[5, p, pl.ds(r + 8, 128)] = (mask_r * w) * F[6, p, pl.ds(r + 8, 128)]
        return carry

    lax.fori_loop(0, 4, own_sweep, 0)

    for q in range(-1, 3):
        def fold0(p, carry, q=q):
            for r in (0, 128):
                at = pl.ds(r + 8, 128)
                if q == -1:
                    s, far = Z[0, p, at], Z[1, p, at]
                elif q == 2:
                    s, far = Z[5, p, at], Z[4, p, at]
                else:
                    s = Z[2 * q + 1, p, at] + Z[2 * q + 2, p, at]
                    far = Z[2 * q, p, at] + Z[2 * q + 3, p, at]
                S0[p, at] = s
                M0[p, at] = (keep + 2.0 * w) * s + w * far
            return carry

        lax.fori_loop(0, 4, fold0, 0)
        for ph in range(2):
            low = fold_lanes(*fold_rows(S0, M0, (2 * ph,), 128), 1, False)
            high = fold_lanes(*fold_rows(S0, M0, (2 * ph + 1,), 128), 1, True)
            value = jnp.where(lanes_of(low.shape) % 2 == 0, low, high)
            if q == -1:
                value = value * mask_l
            if q == 2:
                value = value * mask_r
            FC[q + 1, ph, pl.ds(8, 128)] = value

    pl.semaphore_wait(barrier, n - 1 + groups - 1)
    halo(0, "start")
    halo(1, "start")
    halo(2, "start")
    halo(3, "start")

    for ph in range(2):
        at = pl.ds(8, 128)
        H[1, ph, at] = (mask_l * w) * FC[0, ph, at]
        H[6, ph, at] = (mask_r * w) * FC[3, ph, at]
        for i in range(-1, 3):
            middle, sides = plane_sum(FC, (i + 1, ph), 0, 128, 2)
            if i > -1:
                sides = sides + FC[i, ph, at]
            if i < 2:
                sides = sides + FC[i + 2, ph, at]
            value = keep * middle + w * sides
            if i == -1:
                value = value * mask_l
            if i == 2:
                value = value * mask_r
            H[i + 3, ph, at] = value

    parts = []
    for q in range(-2, 3):
        for ph in range(2):
            at = pl.ds(8, 128)
            lo, hi = 2 * q, 2 * q + 1
            pick = lambda i: H[i + 3, ph, at] if -2 <= i <= 3 else None
            both = [v for v in (pick(lo), pick(hi)) if v is not None]
            ends = [v for v in (pick(lo - 1), pick(hi + 1)) if v is not None]
            s = sum(both[1:], both[0]) if both else jnp.zeros((128, 128), f32)
            far = sum(ends[1:], ends[0])
            S1[ph, at] = s
            M1[ph, at] = (keep + 2.0 * w) * s + w * far
        low = fold_lanes(*fold_rows(S1, M1, (0,), 64), 2, False)
        high = fold_lanes(*fold_rows(S1, M1, (1,), 64), 2, True)
        parts.append(jnp.where(lanes_of(low.shape) % 4 < 2, low, high))
    sy, sz = sy_ref[...], sz_ref[...]
    highest = lax.Precision.HIGHEST
    wide = jnp.dot(sy, jnp.concatenate(parts, 1), precision=highest, preferred_element_type=f32)
    tall = jnp.concatenate([wide[:, 128 * j: 128 * j + 128] for j in range(5)], 0)
    WB[...] = jnp.dot(tall, sz, precision=highest, preferred_element_type=f32)
    for d in range(n):
        for j in range(5):
            SPEC[d, j] = WB[pl.ds(64 * j + 2 * d, 2)]
    REC[me + 2] = SPEC[me]

    each(n, dom_at, go1, "start")
    each(groups, pair_at, go_id, "start")

    halo(4, "start")
    halo(5, "start")

    base = diag_ref[me]

    def pivot(x, before):
        value = 1.0 / (base - before)
        INV[x] = value
        return value

    lax.fori_loop(0, n, pivot, jnp.zeros((2, 128), f32))

    halo(0, "wait_recv")
    halo(1, "wait_recv")
    for ph in range(2):
        for i, side in ((0, CL), (1, CR)):
            value = FC[i + 1, ph, in1] + side[ph]
            X1[i + 4, ph, in1] = value
            X16[i, ph] = value.astype(bf16)
    halo(8, "start")
    halo(9, "start")

    all1("wait_recv")
    for k in (8, 9):
        halo(k, "wait_recv")
    for k in (10, 11):
        halo(k, "start")

    def forward(x, before):
        value = before
        for j in range(5):
            value = value + REC[x + 4 - j, j]
        value = value * INV[x]
        D[x] = value
        return value

    lax.fori_loop(0, n, forward, jnp.zeros((2, 128), f32))

    def backward(i, after):
        x = n - 1 - i
        value = D[x] + INV[x] * after
        UP[x + 2] = value
        return value

    lax.fori_loop(0, n, backward, jnp.zeros((2, 128), f32))
    REC2[me] = UP[pl.ds(me, 5)]
    each(n, dom_at, go2, "start")
    for k in (6, 7):
        halo(k, "start")

    for k in range(2, 6):
        halo(k, "wait_recv")

    def widen(p, carry):
        for x in (1, 2):
            F[x, p, in0] = HL[x, p].astype(f32)
            F[x + 6, p, in0] = HR[x - 1, p].astype(f32)
        return carry

    lax.fori_loop(0, 4, widen, 0)

    def mask0(x):
        at = 4 * me + x
        return jnp.where((at >= 0) & (at < 4 * n), 1.0, 0.0).astype(f32)

    def sweep_y(i, carry):
        x, p = i // 4 - 2, lax.rem(i, 4)
        for r in (0, 128):
            at = pl.ds(r + 8, 128)
            middle, sides = plane_sum(F, (x + 3, p), r, 128, 1)
            sides = sides + F[x + 2, p, at] + F[x + 4, p, at]
            Y[x + 2, p, at] = (w * (1.0 + keep)) * middle + (w * w) * sides
        return carry

    lax.fori_loop(4, 28, sweep_y, 0)

    halo(10, "wait_recv")
    halo(11, "wait_recv")
    for i in range(2):
        for ph in range(2):
            X1[i + 2, ph, in1] = AL[i, ph].astype(f32)
            X1[i + 6, ph, in1] = AR[i, ph].astype(f32)
            X1[i, ph, in1] = BL[i, ph].astype(f32)
            X1[i + 8, ph, in1] = BR[i, ph].astype(f32)

    all2("wait_recv")
    for d in range(n):
        for j in range(5):
            WB[pl.ds(64 * j + 2 * d, 2)] = REC2[d, j]
    tall = jnp.dot(WB[...], sz, precision=highest, preferred_element_type=f32)
    wide = jnp.concatenate([tall[64 * j: 64 * j + 64] for j in range(5)], 1)
    wide = jnp.dot(sy, wide, precision=highest, preferred_element_type=f32)
    for j in range(5):
        U5[j] = wide[:, 128 * j: 128 * j + 128]

    def mask1(i):
        at = 2 * me + i
        return jnp.where((at >= 0) & (at < 2 * n), 1.0, 0.0).astype(f32)

    for ph in range(2):
        for i in range(-3, 5):
            middle, sides = plane_sum(X1, (i + 4, ph), 0, 128, 2)
            sides = sides + X1[i + 3, ph, in1] + X1[i + 5, ph, in1]
            H[i + 3, ph, in1] = (w * (1.0 + keep)) * middle + (w * w) * sides
        for j in range(-2, 3):
            u = U5[j + 2]
            lane = lanes_of(u.shape)
            if ph == 0:
                spread = jnp.where(lane % 4 < 2, u, turn(u, 2))
            else:
                spread = jnp.where(lane % 4 < 2, turn(u, -2), u)
            for i in (2 * j, 2 * j + 1):
                if -3 <= i < 5:
                    for odd in (8, 9):
                        at = pl.ds(odd, 64, stride=2)
                        H[i + 3, ph, at] = H[i + 3, ph, at] + spread
        for i in (-3, -2, -1, 2, 3, 4):
            H[i + 3, ph, in1] = H[i + 3, ph, in1] * mask1(i)
        for i in range(-2, 4):
            middle, sides = plane_sum(H, (i + 3, ph), 0, 128, 2)
            sides = sides + H[i + 2, ph, in1] + H[i + 4, ph, in1]
            value = keep * middle + w * (sides + X1[i + 4, ph, in1])
            Z1[i + 2, ph, in1] = value * mask1(i)
        for i in range(-1, 3):
            middle, sides = plane_sum(Z1, (i + 2, ph), 0, 128, 2)
            sides = sides + Z1[i + 1, ph, in1] + Z1[i + 3, ph, in1]
            value = keep * middle + w * (sides + X1[i + 4, ph, in1])
            V1[i + 1, ph] = value * mask1(i)

    halo(6, "wait_recv")
    halo(7, "wait_recv")

    def widen_far(p, carry):
        F[0, p, in0] = HL[0, p].astype(f32)
        F[9, p, in0] = HR[2, p].astype(f32)
        return carry

    lax.fori_loop(0, 4, widen_far, 0)
    lax.fori_loop(0, 4, sweep_y, 0)
    lax.fori_loop(28, 32, sweep_y, 0)

    def add_coarse(j, carry):
        for p in range(4):
            for r in (0, 64):
                v = V1[j, p // 2, pl.ds(r, 64)]
                even = lanes_of(v.shape) % 2 == 0
                if p % 2 == 0:
                    spread = jnp.where(even, v, turn(v, 1))
                else:
                    spread = jnp.where(even, turn(v, -1), v)
                for x in range(2):
                    for odd in (8, 9):
                        at = pl.ds(2 * r + odd, 64, stride=2)
                        Y[2 * j + x, p, at] = Y[2 * j + x, p, at] + spread
        return carry

    lax.fori_loop(0, 4, add_coarse, 0)

    @pl.when(first)
    def _():
        Y[pl.ds(0, 2)] = jnp.zeros((2, 4, 272, 128), f32)

    @pl.when(last)
    def _():
        Y[pl.ds(6, 2)] = jnp.zeros((2, 4, 272, 128), f32)

    def sweep_z(i, carry):
        x, p = i // 4 - 1, lax.rem(i, 4)
        mask = mask0(x)
        for r in (0, 128):
            at = pl.ds(r + 8, 128)
            middle, sides = plane_sum(Y, (x + 2, p), r, 128, 1)
            sides = sides + Y[x + 1, p, at] + Y[x + 3, p, at]
            Z[x + 1, p, at] = (keep * middle + w * (sides + F[x + 3, p, at])) * mask
        return carry

    lax.fori_loop(0, 24, sweep_z, 0)

    def sweep_out(i, carry):
        x, p = i // 4, lax.rem(i, 4)
        for r in (0, 128):
            at = pl.ds(r + 8, 128)
            middle, sides = plane_sum(Z, (x + 1, p), r, 128, 1)
            sides = sides + Z[x, p, at] + Z[x + 2, p, at]
            value = keep * middle + w * (sides + F[x + 3, p, at])
            pot_ref[p, x, pl.ds(r, 128)] = value.astype(bf16)
        return carry

    lax.fori_loop(0, 16, sweep_out, 0)

    each(groups, pair_at, come_id, "wait_recv")
    copy = pltpu.make_async_copy(IDR, IDS, loc)
    copy.start()
    copy.wait()

    def panel_rows(turn_at, carry):
        far = 0
        for i, offset in enumerate((4, 5, 3, 2, 6, 7, 1)):
            far = jnp.where(turn_at == i, offset, far)
        g = lax.rem(me // 4 + far, groups)
        at_o = [IDS[g, i, 0] for i in range(4)]
        at_v = [IDS[g, i, 1] for i in range(4)]

        def cells(c, sums):
            x, r = c // 8, lax.rem(c, 8) * 32
            at = pl.ds(pl.multiple_of(r, 32), 32)
            pots = [pot_ref[q, x, at].astype(f32) for q in range(4)]
            new = []
            for i in range(4):
                rho = (occ[at_o[i], x, at] * vir[at_v[i], x, at]).astype(f32)
                for q in range(4):
                    product = rho * pots[q]
                    new.append(sums[4 * i + q] + jnp.sum(product.reshape(4, 8, 128), 0))
            return tuple(new)

        sums = lax.fori_loop(0, 32, cells, tuple(jnp.zeros((8, 128), f32) for _ in range(16)))
        for i in range(4):
            rows = [jnp.sum(sums[4 * i + q], 0, keepdims=True) for q in range(4)]
            PART[4 * g + i] = jnp.concatenate(rows, 0)
        for i in range(4):

            @pl.when(4 * g + i != me)
            def _(i=i):
                go3(4 * g + i).start()

        return carry

    lax.fori_loop(0, groups, panel_rows, 0)
    REC3[me] = PART[me]
    all3("wait_recv")
    total = lax.fori_loop(0, n, lambda s, t: t + REC3[s], jnp.zeros((4, 128), f32))
    total = jnp.concatenate([total, jnp.zeros((4, 128), f32)], 0)
    row_sums = lax.dot_general(
        jnp.ones((8, 128), f32), total, (((1,), (1,)), ((), ())), precision=highest, preferred_element_type=f32
    )
    panel_ref[...] = row_sums[0:1, 0:4] / float(4 * 256 * 128 * n)

    for k in range(len(halos)):
        halo(k, "wait_send")
    all1("wait_send")
    all2("wait_send")
    all3("wait_send")
    each(groups, pair_at, go_id, "wait_send")


def tables():
    def sines(length):
        steps = np.arange(length, dtype=np.float64) + 1.0
        return np.sqrt(2.0 / (length + 1)) * np.sin(math.pi * steps[:, None] * steps[None, :] / (length + 1))

    def lams(length):
        return 2.0 - 2.0 * np.cos(math.pi * (np.arange(length, dtype=np.float64) + 1.0) / (length + 1))

    sy = sines(64).astype(np.float32)
    sz = np.kron(sines(32), np.eye(4)).astype(np.float32)
    diag = 2.0 + lams(64)[:, None] + np.repeat(lams(32), 4)[None, :]
    return sy, sz, diag.astype(np.float32).reshape(32, 2, 128)


def solution(mesh):
    n, groups = mesh.shape["dom"], mesh.shape["pair"]
    sy, sz, diag = tables()
    dma, vm = pltpu.SemaphoreType.DMA, pltpu.VMEM
    whole = pl.BlockSpec(memory_space=pltpu.VMEM)

    def shards(occupied, virtual, pair_ids):
        return pl.pallas_call(
            functools.partial(kernel, n, groups),
            out_shape=(
                jax.ShapeDtypeStruct((4, 4, 256, 128), bf16),
                jax.ShapeDtypeStruct((1, 4), f32),
            ),
            in_specs=[pl.BlockSpec(memory_space=pl.ANY)] * 3 + [whole] * 3,
            out_specs=(whole, whole),
            scratch_shapes=[
                vm((12, 4, 256, 128), bf16),
                vm((12, 4, 256, 128), bf16),
                pltpu.SMEM((4, 2), jnp.int32),
                vm((10, 4, 272, 128), f32),
                vm((6, 4, 272, 128), f32),
                vm((8, 4, 272, 128), f32),
                vm((4, 272, 128), f32),
                vm((4, 272, 128), f32),
                vm((10, 2, 144, 128), f32),
                vm((4, 2, 144, 128), f32),
                vm((8, 2, 144, 128), f32),
                vm((6, 2, 144, 128), f32),
                vm((4, 2, 128, 128), f32),
                vm((2, 144, 128), f32),
                vm((2, 144, 128), f32),
                vm((n, 5, 2, 128), f32),
                vm((n + 4, 5, 2, 128), f32),
                vm((n, 2, 128), f32),
                vm((n, 2, 128), f32),
                vm((n + 4, 2, 128), f32),
                vm((n, 5, 2, 128), f32),
                vm((320, 128), f32),
                vm((5, 64, 128), f32),
                vm((2, 128, 128), f32),
                vm((2, 128, 128), f32),
                vm((4, 4, 256, 128), bf16),
                vm((3, 4, 256, 128), bf16),
                vm((3, 4, 256, 128), bf16),
                vm((2, 2, 128, 128), bf16),
                vm((2, 2, 128, 128), bf16),
                vm((2, 2, 128, 128), bf16),
                vm((2, 2, 128, 128), bf16),
                vm((2, 2, 128, 128), bf16),
                vm((n, 4, 128), f32),
                vm((n, 4, 128), f32),
                vm((8, 128), jnp.int32),
                vm((groups, 8, 128), jnp.int32),
                pltpu.SMEM((groups, 8, 128), jnp.int32),
                dma(()), dma(()), dma(()), dma(()), dma(()), dma(()),
                dma((groups,)), dma((groups,)),
                dma((12,)), dma((12,)), dma(()), dma((4,)), dma((4,)), dma(()),
            ],
            compiler_params=pltpu.CompilerParams(
                collective_id=0, has_side_effects=True, vmem_limit_bytes=56 << 20
            ),
            name="casida",
        )(pair_ids, occupied, virtual, jnp.asarray(sy), jnp.asarray(sz), jnp.asarray(diag))

    return jax.shard_map(
        shards,
        mesh=mesh,
        in_specs=(P(None, "dom", None, None), P(None, "dom", None, None), P("pair", None)),
        out_specs=(P("pair", "dom", None, None), P("dom", "pair")),
        check_vma=False,
    )
```

```python
import functools
import math

import jax
import jax.numpy as jnp
import numpy as np
from jax import lax
from jax.experimental import pallas as pl
from jax.experimental.pallas import tpu as pltpu
from jax.sharding import PartitionSpec as P

MESH = pl.DeviceIdType.MESH
f32 = jnp.float32
bf16 = jnp.bfloat16

w = 0.8 / 6.0
keep = 1.0 - 0.8


def lanes_of(shape):
    return lax.broadcasted_iota(jnp.int32, shape, len(shape) - 1)


def turn(value, amount):
    return pltpu.roll(value, amount % 128, value.ndim - 1)


def beside_z(value, step):
    lane = lanes_of(value.shape)
    low = jnp.where(lane >= step, turn(value, step), 0.0)
    high = jnp.where(lane < 128 - step, turn(value, -step), 0.0)
    return low + high


def plane_sum(ref, at, first, rows, step):
    middle = ref[at + (pl.ds(first + 8, rows),)]
    above = ref[at + (pl.ds(first + 7, rows),)]
    below = ref[at + (pl.ds(first + 9, rows),)]
    return middle, above + below + beside_z(middle, step)


def fold_rows(sums, mixed, at, rows):
    even = sums[at + (pl.ds(8, rows, stride=2),)]
    odd = sums[at + (pl.ds(9, rows, stride=2),)]
    before = sums[at + (pl.ds(7, rows, stride=2),)]
    after = sums[at + (pl.ds(10, rows, stride=2),)]
    folded = even + odd
    weighted = mixed[at + (pl.ds(8, rows, stride=2),)] + mixed[at + (pl.ds(9, rows, stride=2),)]
    return folded, weighted + w * (folded + before + after)


def fold_lanes(folded, weighted, step, upper):
    lane = lanes_of(folded.shape)
    if upper:
        total = weighted + turn(weighted, step)
        low, high = turn(folded, 2 * step), turn(folded, -step)
    else:
        total = weighted + turn(weighted, -step)
        low, high = turn(folded, step), turn(folded, -2 * step)
    low = jnp.where(lane >= 2 * step, low, 0.0)
    high = jnp.where(lane < 128 - 2 * step, high, 0.0)
    return 0.5 * (total + w * (low + high))


def zero_rows(ref, lead, total):
    zeros = jnp.zeros((8, 128), f32)
    for at in np.ndindex(*lead):
        ref[at + (pl.ds(0, 8),)] = zeros
        ref[at + (pl.ds(total - 8, 8),)] = zeros


def kernel(n, groups, ids_hbm, occ_hbm, vir_hbm, sy_ref, sz_ref, diag_ref, pot_ref, panel_ref,
           occ, vir, ids_ref, F, Z, Y, S0, M0, X1, FC, H, Z1, V1, S1, M1, SPEC, REC, D, INV, UP, REC2, WB, U5,
           CL, CR, F16, HL, HR, X16, AL, AR, BL, BR, PART, REC3, IDV, IDR, IDS,
           s1, r1, s2, r2, s3, r3, s_id, r_id, s_h, r_h, loc, in_o, in_v, in_id):
    me = lax.axis_index("dom")
    group = lax.axis_index("pair")
    barrier = pltpu.get_barrier_semaphore()

    def dom_at(i):
        return lax.rem(me + i, n)

    def pair_at(i):
        return lax.rem(group + i, groups)

    def signal_dom(i, carry):
        pl.semaphore_signal(barrier, inc=1, device_id={"dom": dom_at(i)}, device_id_type=MESH)
        return carry

    def signal_pair(i, carry):
        pl.semaphore_signal(barrier, inc=1, device_id={"pair": pair_at(i)}, device_id_type=MESH)
        return carry

    lax.fori_loop(1, n, signal_dom, 0)
    lax.fori_loop(1, groups, signal_pair, 0)

    ids_in = pltpu.make_async_copy(ids_hbm, ids_ref, in_id)
    ids_in.start()
    loads = []
    for x in range(4):
        loads.append(pltpu.make_async_copy(occ_hbm.at[:, x], occ.at[:, x], in_o.at[x]))
        loads.append(pltpu.make_async_copy(vir_hbm.at[:, x], vir.at[:, x], in_v.at[x]))
    for load in loads:
        load.start()

    first, last = me == 0, me == n - 1
    inner_l, inner_r = me > 0, me < n - 1
    mask_l = jnp.where(inner_l, 1.0, 0.0).astype(f32)
    mask_r = jnp.where(inner_r, 1.0, 0.0).astype(f32)

    zero_rows(F, (10, 4), 272)
    zero_rows(Z, (6, 4), 272)
    zero_rows(Y, (8, 4), 272)
    zero_rows(S0, (4,), 272)
    zero_rows(X1, (10, 2), 144)
    zero_rows(FC, (4, 2), 144)
    zero_rows(H, (8, 2), 144)
    zero_rows(Z1, (6, 2), 144)
    zero_rows(S1, (2,), 144)
    UP[pl.ds(0, 2)] = jnp.zeros((2, 2, 128), f32)
    UP[pl.ds(n + 2, 2)] = jnp.zeros((2, 2, 128), f32)
    REC[pl.ds(0, 2)] = jnp.zeros((2, 5, 2, 128), f32)
    REC[pl.ds(n + 2, 2)] = jnp.zeros((2, 5, 2, 128), f32)

    @pl.when(first)
    def _():
        HL[...] = jnp.zeros((3, 4, 256, 128), bf16)
        AL[...] = jnp.zeros((2, 2, 128, 128), bf16)
        BL[...] = jnp.zeros((2, 2, 128, 128), bf16)
        CL[...] = jnp.zeros((2, 128, 128), f32)

    @pl.when(last)
    def _():
        HR[...] = jnp.zeros((3, 4, 256, 128), bf16)
        AR[...] = jnp.zeros((2, 2, 128, 128), bf16)
        BR[...] = jnp.zeros((2, 2, 128, 128), bf16)
        CR[...] = jnp.zeros((2, 128, 128), f32)

    ids_in.wait()

    row = lax.broadcasted_iota(jnp.int32, (8, 128), 0)
    col = lax.broadcasted_iota(jnp.int32, (8, 128), 1)
    own_ids = jnp.zeros((8, 128), jnp.int32)
    for i in range(4):
        for c in range(2):
            own_ids = jnp.where((row == i) & (col == c), ids_ref[i, c], own_ids)
    IDV[...] = own_ids
    IDR[group] = own_ids

    for load in loads:
        load.wait()
    for p in range(4):
        io, iv = ids_ref[p, 0], ids_ref[p, 1]

        def density(x, carry, p=p, io=io, iv=iv):
            rho = occ[io, x].astype(f32) * vir[iv, x].astype(f32)
            F[x + 3, p, pl.ds(8, 256)] = rho
            F16[x, p] = rho.astype(bf16)
            return carry

        lax.fori_loop(0, 4, density, 0)


    def remote(src, dst, send, recv, where):
        return pltpu.make_async_remote_copy(
            src_ref=src, dst_ref=dst, send_sem=send, recv_sem=recv, device_id=where, device_id_type=MESH
        )

    def go1(t):
        return remote(SPEC.at[t], REC.at[me + 2], s1, r1, {"dom": t})

    others = pl.ds(0, n - 1)

    def all1(what):
        part = SPEC.at[others]
        getattr(remote(part, part, s1, r1, {"dom": dom_at(1)}), what)()

    def all2(what):
        part = REC2.at[others]
        getattr(remote(part, part, s2, r2, {"dom": dom_at(1)}), what)()

    def all3(what):
        part = PART.at[others]
        getattr(remote(part, part, s3, r3, {"dom": dom_at(1)}), what)()

    def go2(t):
        return remote(UP.at[pl.ds(t, 5)], REC2.at[me], s2, r2, {"dom": t})

    def go3(t):
        return remote(PART.at[t], REC3.at[me], s3, r3, {"dom": t})

    def go_id(t):
        return remote(IDV, IDR.at[group], s_id.at[t], r_id.at[group], {"pair": t})

    def come_id(s):
        return remote(IDV, IDR.at[s], s_id.at[s], r_id.at[s], {"pair": s})

    def each(count, at, build, what):
        def body(i, carry):
            getattr(build(at(i)), what)()
            return carry

        lax.fori_loop(1, count, body, 0)

    in0, in1 = pl.ds(8, 256), pl.ds(8, 128)
    halos = [
        (FC.at[3, :, in1], CL, 1),
        (FC.at[0, :, in1], CR, -1),
        (F16.at[3], HL.at[2], 1),
        (F16.at[0], HR.at[0], -1),
        (F16.at[2], HL.at[1], 1),
        (F16.at[1], HR.at[1], -1),
        (F16.at[1], HL.at[0], 1),
        (F16.at[2], HR.at[2], -1),
        (X16, AL, 1),
        (X16, AR, -1),
        (AL, BL, 1),
        (AR, BR, -1),
    ]

    def halo(k, what):
        src, dst, off = halos[k]
        outgoing = what in ("start", "wait_send")
        towards = off if outgoing else -off
        there = (me < n - towards) if towards > 0 else (me >= -towards)

        @pl.when(there)
        def _():
            copy = remote(src, dst, s_h.at[k], r_h.at[k], {"dom": lax.rem(me + off + n, n)})
            getattr(copy, what)()

    def own_sweep(p, carry):
        for r in (0, 128):
            for x in range(4):
                middle, sides = plane_sum(F, (x + 3, p), r, 128, 1)
                if x > 0:
                    sides = sides + F[x + 2, p, pl.ds(r + 8, 128)]
                if x < 3:
                    sides = sides + F[x + 4, p, pl.ds(r + 8, 128)]
                Z[x + 1, p, pl.ds(r + 8, 128)] = keep * middle + w * sides
            Z[0, p, pl.ds(r + 8, 128)] = (mask_l * w) * F[3, p, pl.ds(r + 8, 128)]
            Z[5, p, pl.ds(r + 8, 128)] = (mask_r * w) * F[6, p, pl.ds(r + 8, 128)]
        return carry

    lax.fori_loop(0, 4, own_sweep, 0)

    for q in range(-1, 3):
        def fold0(p, carry, q=q):
            for r in (0, 128):
                at = pl.ds(r + 8, 128)
                if q == -1:
                    s, far = Z[0, p, at], Z[1, p, at]
                elif q == 2:
                    s, far = Z[5, p, at], Z[4, p, at]
                else:
                    s = Z[2 * q + 1, p, at] + Z[2 * q + 2, p, at]
                    far = Z[2 * q, p, at] + Z[2 * q + 3, p, at]
                S0[p, at] = s
                M0[p, at] = (keep + 2.0 * w) * s + w * far
            return carry

        lax.fori_loop(0, 4, fold0, 0)
        for ph in range(2):
            low = fold_lanes(*fold_rows(S0, M0, (2 * ph,), 128), 1, False)
            high = fold_lanes(*fold_rows(S0, M0, (2 * ph + 1,), 128), 1, True)
            value = jnp.where(lanes_of(low.shape) % 2 == 0, low, high)
            if q == -1:
                value = value * mask_l
            if q == 2:
                value = value * mask_r
            FC[q + 1, ph, pl.ds(8, 128)] = value

    pl.semaphore_wait(barrier, n - 1 + groups - 1)
    halo(0, "start")
    halo(1, "start")
    halo(2, "start")
    halo(3, "start")

    for ph in range(2):
        at = pl.ds(8, 128)
        H[1, ph, at] = (mask_l * w) * FC[0, ph, at]
        H[6, ph, at] = (mask_r * w) * FC[3, ph, at]
        for i in range(-1, 3):
            middle, sides = plane_sum(FC, (i + 1, ph), 0, 128, 2)
            if i > -1:
                sides = sides + FC[i, ph, at]
            if i < 2:
                sides = sides + FC[i + 2, ph, at]
            value = keep * middle + w * sides
            if i == -1:
                value = value * mask_l
            if i == 2:
                value = value * mask_r
            H[i + 3, ph, at] = value

    parts = []
    for q in range(-2, 3):
        for ph in range(2):
            at = pl.ds(8, 128)
            lo, hi = 2 * q, 2 * q + 1
            pick = lambda i: H[i + 3, ph, at] if -2 <= i <= 3 else None
            both = [v for v in (pick(lo), pick(hi)) if v is not None]
            ends = [v for v in (pick(lo - 1), pick(hi + 1)) if v is not None]
            s = sum(both[1:], both[0]) if both else jnp.zeros((128, 128), f32)
            far = sum(ends[1:], ends[0])
            S1[ph, at] = s
            M1[ph, at] = (keep + 2.0 * w) * s + w * far
        low = fold_lanes(*fold_rows(S1, M1, (0,), 64), 2, False)
        high = fold_lanes(*fold_rows(S1, M1, (1,), 64), 2, True)
        parts.append(jnp.where(lanes_of(low.shape) % 4 < 2, low, high))
    sy, sz = sy_ref[...], sz_ref[...]
    highest = lax.Precision.HIGHEST
    wide = jnp.dot(sy, jnp.concatenate(parts, 1), precision=highest, preferred_element_type=f32)
    tall = jnp.concatenate([wide[:, 128 * j: 128 * j + 128] for j in range(5)], 0)
    WB[...] = jnp.dot(tall, sz, precision=highest, preferred_element_type=f32)
    for d in range(n):
        for j in range(5):
            SPEC[d, j] = WB[pl.ds(64 * j + 2 * d, 2)]
    REC[me + 2] = SPEC[me]

    each(n, dom_at, go1, "start")
    each(groups, pair_at, go_id, "start")

    halo(4, "start")
    halo(5, "start")

    base = diag_ref[me]

    def pivot(x, before):
        value = 1.0 / (base - before)
        INV[x] = value
        return value

    lax.fori_loop(0, n, pivot, jnp.zeros((2, 128), f32))

    halo(0, "wait_recv")
    halo(1, "wait_recv")
    for ph in range(2):
        for i, side in ((0, CL), (1, CR)):
            value = FC[i + 1, ph, in1] + side[ph]
            X1[i + 4, ph, in1] = value
            X16[i, ph] = value.astype(bf16)
    halo(8, "start")
    halo(9, "start")

    all1("wait_recv")
    for k in (8, 9):
        halo(k, "wait_recv")
    for k in (10, 11):
        halo(k, "start")

    def forward(x, before):
        value = before
        for j in range(5):
            value = value + REC[x + 4 - j, j]
        value = value * INV[x]
        D[x] = value
        return value

    lax.fori_loop(0, n, forward, jnp.zeros((2, 128), f32))

    def backward(i, after):
        x = n - 1 - i
        value = D[x] + INV[x] * after
        UP[x + 2] = value
        return value

    lax.fori_loop(0, n, backward, jnp.zeros((2, 128), f32))
    REC2[me] = UP[pl.ds(me, 5)]
    each(n, dom_at, go2, "start")
    for k in (6, 7):
        halo(k, "start")

    for k in range(2, 6):
        halo(k, "wait_recv")

    def widen(p, carry):
        for x in (1, 2):
            F[x, p, in0] = HL[x, p].astype(f32)
            F[x + 6, p, in0] = HR[x - 1, p].astype(f32)
        return carry

    lax.fori_loop(0, 4, widen, 0)

    def mask0(x):
        at = 4 * me + x
        return jnp.where((at >= 0) & (at < 4 * n), 1.0, 0.0).astype(f32)

    def sweep_y(i, carry):
        x, p = i // 4 - 2, lax.rem(i, 4)
        for r in (0, 128):
            at = pl.ds(r + 8, 128)
            middle, sides = plane_sum(F, (x + 3, p), r, 128, 1)
            sides = sides + F[x + 2, p, at] + F[x + 4, p, at]
            Y[x + 2, p, at] = (w * (1.0 + keep)) * middle + (w * w) * sides
        return carry

    lax.fori_loop(4, 28, sweep_y, 0, unroll=2)

    halo(10, "wait_recv")
    halo(11, "wait_recv")
    for i in range(2):
        for ph in range(2):
            X1[i + 2, ph, in1] = AL[i, ph].astype(f32)
            X1[i + 6, ph, in1] = AR[i, ph].astype(f32)
            X1[i, ph, in1] = BL[i, ph].astype(f32)
            X1[i + 8, ph, in1] = BR[i, ph].astype(f32)

    all2("wait_recv")
    for d in range(n):
        for j in range(5):
            WB[pl.ds(64 * j + 2 * d, 2)] = REC2[d, j]
    tall = jnp.dot(WB[...], sz, precision=highest, preferred_element_type=f32)
    wide = jnp.concatenate([tall[64 * j: 64 * j + 64] for j in range(5)], 1)
    wide = jnp.dot(sy, wide, precision=highest, preferred_element_type=f32)
    for j in range(5):
        U5[j] = wide[:, 128 * j: 128 * j + 128]

    def mask1(i):
        at = 2 * me + i
        return jnp.where((at >= 0) & (at < 2 * n), 1.0, 0.0).astype(f32)

    for ph in range(2):
        for i in range(-3, 5):
            middle, sides = plane_sum(X1, (i + 4, ph), 0, 128, 2)
            sides = sides + X1[i + 3, ph, in1] + X1[i + 5, ph, in1]
            H[i + 3, ph, in1] = (w * (1.0 + keep)) * middle + (w * w) * sides
        for j in range(-2, 3):
            u = U5[j + 2]
            lane = lanes_of(u.shape)
            if ph == 0:
                spread = jnp.where(lane % 4 < 2, u, turn(u, 2))
            else:
                spread = jnp.where(lane % 4 < 2, turn(u, -2), u)
            for i in (2 * j, 2 * j + 1):
                if -3 <= i < 5:
                    for odd in (8, 9):
                        at = pl.ds(odd, 64, stride=2)
                        H[i + 3, ph, at] = H[i + 3, ph, at] + spread
        for i in (-3, -2, -1, 2, 3, 4):
            H[i + 3, ph, in1] = H[i + 3, ph, in1] * mask1(i)
        for i in range(-2, 4):
            middle, sides = plane_sum(H, (i + 3, ph), 0, 128, 2)
            sides = sides + H[i + 2, ph, in1] + H[i + 4, ph, in1]
            value = keep * middle + w * (sides + X1[i + 4, ph, in1])
            Z1[i + 2, ph, in1] = value * mask1(i)
        for i in range(-1, 3):
            middle, sides = plane_sum(Z1, (i + 2, ph), 0, 128, 2)
            sides = sides + Z1[i + 1, ph, in1] + Z1[i + 3, ph, in1]
            value = keep * middle + w * (sides + X1[i + 4, ph, in1])
            V1[i + 1, ph] = value * mask1(i)

    halo(6, "wait_recv")
    halo(7, "wait_recv")

    def widen_far(p, carry):
        F[0, p, in0] = HL[0, p].astype(f32)
        F[9, p, in0] = HR[2, p].astype(f32)
        return carry

    lax.fori_loop(0, 4, widen_far, 0)
    lax.fori_loop(0, 4, sweep_y, 0)
    lax.fori_loop(28, 32, sweep_y, 0)

    def add_coarse(j, carry):
        for p in range(4):
            for r in (0, 64):
                v = V1[j, p // 2, pl.ds(r, 64)]
                even = lanes_of(v.shape) % 2 == 0
                if p % 2 == 0:
                    spread = jnp.where(even, v, turn(v, 1))
                else:
                    spread = jnp.where(even, turn(v, -1), v)
                for x in range(2):
                    for odd in (8, 9):
                        at = pl.ds(2 * r + odd, 64, stride=2)
                        Y[2 * j + x, p, at] = Y[2 * j + x, p, at] + spread
        return carry

    lax.fori_loop(0, 4, add_coarse, 0)

    @pl.when(first)
    def _():
        Y[pl.ds(0, 2)] = jnp.zeros((2, 4, 272, 128), f32)

    @pl.when(last)
    def _():
        Y[pl.ds(6, 2)] = jnp.zeros((2, 4, 272, 128), f32)

    def sweep_z(i, carry):
        x, p = i // 4 - 1, lax.rem(i, 4)
        mask = mask0(x)
        for r in (0, 128):
            at = pl.ds(r + 8, 128)
            middle, sides = plane_sum(Y, (x + 2, p), r, 128, 1)
            sides = sides + Y[x + 1, p, at] + Y[x + 3, p, at]
            Z[x + 1, p, at] = (keep * middle + w * (sides + F[x + 3, p, at])) * mask
        return carry

    lax.fori_loop(0, 24, sweep_z, 0, unroll=2)

    def sweep_out(i, carry):
        x, p = i // 4, lax.rem(i, 4)
        for r in (0, 128):
            at = pl.ds(r + 8, 128)
            middle, sides = plane_sum(Z, (x + 1, p), r, 128, 1)
            sides = sides + Z[x, p, at] + Z[x + 2, p, at]
            value = keep * middle + w * (sides + F[x + 3, p, at])
            pot_ref[p, x, pl.ds(r, 128)] = value.astype(bf16)
        return carry

    lax.fori_loop(0, 16, sweep_out, 0, unroll=2)

    each(groups, pair_at, come_id, "wait_recv")
    copy = pltpu.make_async_copy(IDR, IDS, loc)
    copy.start()
    copy.wait()

    def panel_rows(turn_at, carry):
        far = 0
        for i, offset in enumerate((4, 5, 3, 2, 6, 7, 1)):
            far = jnp.where(turn_at == i, offset, far)
        g = lax.rem(me // 4 + far, groups)
        at_o = [IDS[g, i, 0] for i in range(4)]
        at_v = [IDS[g, i, 1] for i in range(4)]

        def cells(c, sums):
            x, r = c // 8, lax.rem(c, 8) * 32
            at = pl.ds(pl.multiple_of(r, 32), 32)
            pots = [pot_ref[q, x, at].astype(f32) for q in range(4)]
            new = []
            for i in range(4):
                rho = (occ[at_o[i], x, at] * vir[at_v[i], x, at]).astype(f32)
                for q in range(4):
                    product = rho * pots[q]
                    new.append(sums[4 * i + q] + jnp.sum(product.reshape(4, 8, 128), 0))
            return tuple(new)

        sums = lax.fori_loop(0, 32, cells, tuple(jnp.zeros((8, 128), f32) for _ in range(16)), unroll=4)
        for i in range(4):
            rows = [jnp.sum(sums[4 * i + q], 0, keepdims=True) for q in range(4)]
            PART[4 * g + i] = jnp.concatenate(rows, 0)
        for i in range(4):

            @pl.when(4 * g + i != me)
            def _(i=i):
                go3(4 * g + i).start()

        return carry

    lax.fori_loop(0, groups, panel_rows, 0)
    REC3[me] = PART[me]
    all3("wait_recv")
    total = lax.fori_loop(0, n, lambda s, t: t + REC3[s], jnp.zeros((4, 128), f32))
    total = jnp.concatenate([total, jnp.zeros((4, 128), f32)], 0)
    row_sums = lax.dot_general(
        jnp.ones((8, 128), f32), total, (((1,), (1,)), ((), ())), precision=highest, preferred_element_type=f32
    )
    panel_ref[...] = row_sums[0:1, 0:4] / float(4 * 256 * 128 * n)

    for k in range(len(halos)):
        halo(k, "wait_send")
    all1("wait_send")
    all2("wait_send")
    all3("wait_send")
    each(groups, pair_at, go_id, "wait_send")


def tables():
    def sines(length):
        steps = np.arange(length, dtype=np.float64) + 1.0
        return np.sqrt(2.0 / (length + 1)) * np.sin(math.pi * steps[:, None] * steps[None, :] / (length + 1))

    def lams(length):
        return 2.0 - 2.0 * np.cos(math.pi * (np.arange(length, dtype=np.float64) + 1.0) / (length + 1))

    sy = sines(64).astype(np.float32)
    sz = np.kron(sines(32), np.eye(4)).astype(np.float32)
    diag = 2.0 + lams(64)[:, None] + np.repeat(lams(32), 4)[None, :]
    return sy, sz, diag.astype(np.float32).reshape(32, 2, 128)


def solution(mesh):
    n, groups = mesh.shape["dom"], mesh.shape["pair"]
    sy, sz, diag = tables()
    dma, vm = pltpu.SemaphoreType.DMA, pltpu.VMEM
    whole = pl.BlockSpec(memory_space=pltpu.VMEM)

    def shards(occupied, virtual, pair_ids):
        return pl.pallas_call(
            functools.partial(kernel, n, groups),
            out_shape=(
                jax.ShapeDtypeStruct((4, 4, 256, 128), bf16),
                jax.ShapeDtypeStruct((1, 4), f32),
            ),
            in_specs=[pl.BlockSpec(memory_space=pl.ANY)] * 3 + [whole] * 3,
            out_specs=(whole, whole),
            scratch_shapes=[
                vm((12, 4, 256, 128), bf16),
                vm((12, 4, 256, 128), bf16),
                pltpu.SMEM((4, 2), jnp.int32),
                vm((10, 4, 272, 128), f32),
                vm((6, 4, 272, 128), f32),
                vm((8, 4, 272, 128), f32),
                vm((4, 272, 128), f32),
                vm((4, 272, 128), f32),
                vm((10, 2, 144, 128), f32),
                vm((4, 2, 144, 128), f32),
                vm((8, 2, 144, 128), f32),
                vm((6, 2, 144, 128), f32),
                vm((4, 2, 128, 128), f32),
                vm((2, 144, 128), f32),
                vm((2, 144, 128), f32),
                vm((n, 5, 2, 128), f32),
                vm((n + 4, 5, 2, 128), f32),
                vm((n, 2, 128), f32),
                vm((n, 2, 128), f32),
                vm((n + 4, 2, 128), f32),
                vm((n, 5, 2, 128), f32),
                vm((320, 128), f32),
                vm((5, 64, 128), f32),
                vm((2, 128, 128), f32),
                vm((2, 128, 128), f32),
                vm((4, 4, 256, 128), bf16),
                vm((3, 4, 256, 128), bf16),
                vm((3, 4, 256, 128), bf16),
                vm((2, 2, 128, 128), bf16),
                vm((2, 2, 128, 128), bf16),
                vm((2, 2, 128, 128), bf16),
                vm((2, 2, 128, 128), bf16),
                vm((2, 2, 128, 128), bf16),
                vm((n, 4, 128), f32),
                vm((n, 4, 128), f32),
                vm((8, 128), jnp.int32),
                vm((groups, 8, 128), jnp.int32),
                pltpu.SMEM((groups, 8, 128), jnp.int32),
                dma(()), dma(()), dma(()), dma(()), dma(()), dma(()),
                dma((groups,)), dma((groups,)),
                dma((12,)), dma((12,)), dma(()), dma((4,)), dma((4,)), dma(()),
            ],
            compiler_params=pltpu.CompilerParams(
                collective_id=0, has_side_effects=True, vmem_limit_bytes=56 << 20
            ),
            name="casida",
        )(pair_ids, occupied, virtual, jnp.asarray(sy), jnp.asarray(sz), jnp.asarray(diag))

    return jax.shard_map(
        shards,
        mesh=mesh,
        in_specs=(P(None, "dom", None, None), P(None, "dom", None, None), P("pair", None)),
        out_specs=(P("pair", "dom", None, None), P("dom", "pair")),
        check_vma=False,
    )
```
